32 devices in a mesh: row: 8 (over z, y), col: 4 (over x, core).
Axes of the slice: x: 2, y: 2, z: 4, core: 2. Of those that a mesh axis runs over, the one named last changes fastest.
Arguments:
- momentum: float32 [8192, 16384], P('row', 'col'), may hold values from -6 to 6
- grads: bfloat16 [2, 8192, 16384], P(None, 'row', 'col'), may hold values from -400 to 400
- basis: float32 [16384, 256], P('col'), may hold values from -0.046875 to 0.046875
Outputs:
- change: bfloat16 [8192, 16384], P('row', 'col')
- state: float32 [8192, 16384], P('row', 'col')
The draws below stay inside these ranges and needn't reach their ends.
All inputs are finite; a program needn't handle non-finite values.
Results may differ from the reference program's by a relative error of at most 0.0035.
Values sent between devices are 32-bit elements; how exact they have to be, the bound alone decides.
A program may use at most 192 MiB of HBM per device.

```python
import jax
import jax.numpy as jnp
from jax import lax

ROWS = 8192
COLS = 16384
RANK = 256
STEPS = 2


def draw_grads(key, part):
    row_key = jax.random.fold_in(key, 11)
    col_key = jax.random.fold_in(key, 12)
    base_key = jax.random.fold_in(key, 13)
    row_scale = jnp.exp(jax.random.uniform(row_key, (1, ROWS, 1), jnp.float32, jnp.log(0.3), jnp.log(3.0)))
    col_scale = jnp.exp(jax.random.uniform(col_key, (1, 1, COLS), jnp.float32, jnp.log(0.3), jnp.log(3.0)))
    values = jax.random.normal(base_key, (STEPS, ROWS, COLS), jnp.float32) * row_scale * col_scale
    return jnp.clip(values, -400.0, 400.0).astype(jnp.bfloat16)


def shard_levels(key, dims, shards, least, high):
    gain = 1.0
    for dim, blocks in shards:
        draws = jax.random.uniform(jax.random.fold_in(jax.random.fold_in(key, 6), dim), (blocks,), jnp.float32, least / len(shards), high / len(shards))
        gain = gain * jnp.repeat(jnp.exp(draws), dims[dim] // blocks).reshape((-1,) + (1,) * (len(dims) - 1 - dim))
    return gain


def gaussian(stream_key, shape, deviation, limit, pieces=(), dtype=jnp.bfloat16):
    gain = shard_levels(stream_key, shape, pieces, -0.22, 0.18) if pieces else 1.0
    entries = jax.random.normal(stream_key, shape, jnp.float32) * deviation * gain
    return jnp.minimum(jnp.maximum(entries, -limit), limit).astype(dtype)


def setup_inputs(seed: int = 0) -> dict:
    arg_keys = jax.random.split(jax.random.key(seed), 4)
    return {
        "momentum": gaussian(arg_keys[0], (ROWS, COLS), 1.0, 6.0, ((0, 8), (1, 4)), jnp.float32),
        "grads": draw_grads(jax.random.fold_in(arg_keys[3], 71), 0),
        "basis": gaussian(arg_keys[2], (COLS, RANK), COLS ** -0.5, 0.046875, ((0, 4),), jnp.float32),
    }


keep_rate = 0.95
norm_eps = 1e-06

def reference(momentum, grads, basis):
    high = lax.Precision.HIGHEST
    factor = (ROWS * COLS / RANK) ** 0.5
    state = momentum
    right = basis
    change = jnp.zeros(momentum.shape, jnp.float32)
    for step in range(STEPS):
        buffer = state + grads[step].astype(jnp.float32)
        projected = jnp.dot(buffer.astype(jnp.float32), right.astype(jnp.float32), precision=high, preferred_element_type=jnp.float32)
        gram = jnp.dot(projected.T.astype(jnp.float32), projected.astype(jnp.float32), precision=high, preferred_element_type=jnp.float32)
        lower = jnp.linalg.cholesky(gram)
        ortho = jax.scipy.linalg.solve_triangular(lower, projected.T, lower=True).T
        raw = lax.dot_general(buffer.astype(jnp.float32), ortho.astype(jnp.float32), (((0,), (0,)), ((), ())), precision=high, preferred_element_type=jnp.float32)
        scale = lax.rsqrt(lax.optimization_barrier(jnp.sum(raw * raw, axis=0)) + norm_eps)
        right = raw * scale
        state = buffer - (1.0 - keep_rate) * jnp.dot(ortho.astype(jnp.float32), raw.T.astype(jnp.float32), precision=high, preferred_element_type=jnp.float32)
        change = change + factor * jnp.dot(ortho.astype(jnp.float32), right.T.astype(jnp.float32), precision=high, preferred_element_type=jnp.float32)
    return (change.astype(jnp.bfloat16), state)
```

```python
import functools

import jax
import jax.numpy as jnp
from jax import lax
from jax.experimental import pallas as pl
from jax.experimental.pallas import tpu as pltpu
from jax.sharding import PartitionSpec as P

keep_rate = 0.95
norm_eps = 1e-06
HIGH = lax.Precision.HIGH
HIGHEST = lax.Precision.HIGHEST
MESH = pl.DeviceIdType.MESH
LANES = 128
STRIDE = 2


def matmul(a, b, dims, precision):
    return lax.dot_general(a, b, (dims, ((), ())), precision=precision, preferred_element_type=jnp.float32)


def split(x):
    high = x.astype(jnp.bfloat16)
    return high, (x - high.astype(jnp.float32)).astype(jnp.bfloat16)


def reduce_kernel(axis, orders, count, *refs):
    bits = range(len(orders[0]))
    inputs, outs, recvs, works = (refs[k * count : (k + 1) * count] for k in range(4))
    send_sem, recv_sem = refs[4 * count :]
    me = lax.axis_index(axis)
    halves = [lax.rem(me // (1 << b), 2) for b in bits]
    partners = [me + (1 - 2 * h) * (1 << b) for h, b in zip(halves, bits)]
    barrier = pltpu.get_barrier_semaphore()
    for p in partners:
        pl.semaphore_signal(barrier, inc=1, device_id={axis: p}, device_id_type=pl.DeviceIdType.MESH)
    pl.semaphore_wait(barrier, len(bits))

    starts = [[0] for _ in range(count)]
    for s in range(len(bits)):
        copies = []
        for i in range(count):
            size = inputs[i].shape[0] >> (s + 1)
            base = inputs[i].shape[0] - 2 * size
            source = inputs[i] if s == 0 else works[i]
            there = pl.multiple_of(starts[i][s] + (1 - halves[orders[i][s]]) * size, 8)
            copy = pltpu.make_async_remote_copy(
                src_ref=source.at[pl.ds(there, size)],
                dst_ref=recvs[i].at[pl.ds(base, size)],
                send_sem=send_sem.at[i, s],
                recv_sem=recv_sem.at[i, s],
                device_id={axis: partners[orders[i][s]]},
                device_id_type=pl.DeviceIdType.MESH,
            )
            copy.start()
            copies.append(copy)
        for i in range(count):
            size = inputs[i].shape[0] >> (s + 1)
            base = inputs[i].shape[0] - 2 * size
            source = inputs[i] if s == 0 else works[i]
            here = pl.multiple_of(starts[i][s] + halves[orders[i][s]] * size, 8)
            copies[i].wait()
            target = outs[i] if s == len(bits) - 1 else works[i]
            target[pl.ds(here, size), :] = source[pl.ds(here, size), :] + recvs[i][pl.ds(base, size), :]
            starts[i].append(here)
    for s in reversed(range(len(bits))):
        t = 2 * len(bits) - 1 - s
        copies = []
        for i in range(count):
            size = inputs[i].shape[0] >> (s + 1)
            mine = outs[i].at[pl.ds(starts[i][s + 1], size)]
            copy = pltpu.make_async_remote_copy(
                src_ref=mine,
                dst_ref=mine,
                send_sem=send_sem.at[i, t],
                recv_sem=recv_sem.at[i, t],
                device_id={axis: partners[orders[i][s]]},
                device_id_type=pl.DeviceIdType.MESH,
            )
            copy.start()
            copies.append(copy)
        for copy in copies:
            copy.wait()


def all_reduce(arrays, axis, size, collective_id):
    bits = list(range(size.bit_length() - 1))
    count = len(arrays)
    orders = [bits[t:] + bits[:t] for t in (min(1, max(0, i - 1)) for i in range(count))]
    total = sum(a.size for a in arrays)
    vmem = pl.BlockSpec(memory_space=pltpu.VMEM)
    return pl.pallas_call(
        functools.partial(reduce_kernel, axis, orders, count),
        out_shape=[jax.ShapeDtypeStruct(a.shape, a.dtype) for a in arrays],
        in_specs=[vmem] * count,
        out_specs=[vmem] * count,
        scratch_shapes=[pltpu.VMEM(a.shape, a.dtype) for a in arrays * 2]
        + [pltpu.SemaphoreType.DMA((count, 2 * len(bits))), pltpu.SemaphoreType.DMA((count, 2 * len(bits)))],
        compiler_params=pltpu.CompilerParams(
            collective_id=collective_id, has_side_effects=True, vmem_limit_bytes=16 * 2**20
        ),
        cost_estimate=pl.CostEstimate(flops=total, bytes_accessed=40 * total, transcendentals=0),
    )(*arrays)


KINDS = 11


def row_kernel(rows, step, state, grads, projected, fin, inverse, work, outer, middle, pair, turned, factor, panel,
               states, slopes, load_sem, send_sem, recv_sem):
    half = rows // 4
    rank = inverse.shape[0]
    first = rank // LANES
    chunks = fin.shape[0]
    size = rank // 8
    me = lax.axis_index("row")
    y = lax.rem(me, 2)
    z = me // 2
    left = z < half
    depth = jnp.where(left, z, 2 * half - 1 - z)
    is_middle = depth == half - 1
    is_end = depth == 0
    inward = jnp.where(left, me + 2, me - 2)
    outward = jnp.where(left, me - 2, me + 2)
    partner = me + 1 - 2 * y
    mine = pl.multiple_of(2 * size * y, 8)
    yours = pl.multiple_of(2 * size * (1 - y), 8)
    side = jnp.where(left, 0, 1)
    near1 = pl.multiple_of(mine + size * side, 8)
    far1 = pl.multiple_of(mine + size * (1 - side), 8)
    near2 = pl.multiple_of(4 * size + 2 * size * side, 8)
    far2 = pl.multiple_of(4 * size + 2 * size * (1 - side), 8)

    def load(j, slot):
        columns = pl.ds(pl.multiple_of(j * LANES, LANES), LANES)
        return (
            pltpu.make_async_copy(state.at[:, columns], states.at[slot], load_sem.at[0, slot]),
            pltpu.make_async_copy(grads.at[step, :, columns], slopes.at[slot], load_sem.at[1, slot]),
        )

    for copy in load(0, 0):
        copy.start()

    def send(kind, c, source, start, target, at, count, device):
        return pltpu.make_async_remote_copy(
            src_ref=source.at[c, pl.ds(start, count)],
            dst_ref=target.at[c, pl.ds(at, count)],
            send_sem=send_sem.at[kind, c],
            recv_sem=recv_sem.at[kind, c],
            device_id={"row": device},
            device_id_type=MESH,
        )

    copies = {
        0: lambda c: send(0, c, work, yours, pair, 0, 2 * size, partner),
        1: lambda c: send(1, c, work, mine, outer, 0, 2 * size, inward),
        2: lambda c: send(2, c, work, 4 * size, outer, 2 * size, 4 * size, inward),
        3: lambda c: send(3, c, work, far1, middle, 0, size, inward),
        4: lambda c: send(4, c, work, far2, middle, size, 2 * size, inward),
        5: lambda c: send(5, c, work, near2, pair, 2 * size, 2 * size, partner),
        6: lambda c: send(6, c, fin, near1, fin, near1, size, inward),
        7: lambda c: send(7, c, fin, near2, fin, near2, 2 * size, inward),
        8: lambda c: send(8, c, fin, mine, fin, mine, 2 * size, outward),
        9: lambda c: send(9, c, fin, 4 * size, fin, 4 * size, 4 * size, outward),
        10: lambda c: send(10, c, fin, mine, fin, mine, 2 * size, partner),
    }

    def add(target, c, start, source, at, count, base=work):
        target[c, pl.ds(start, count), :] = base[c, pl.ds(start, count), :] + source[c, pl.ds(at, count), :]

    transposed = projected[...].T
    high, low = split(transposed)
    turned[0] = high
    turned[1] = low
    gram = matmul(transposed, transposed, ((1,), (1,)), HIGHEST)
    for k in range(first):
        work[k] = gram[:, k * LANES : (k + 1) * LANES]

    barrier = pltpu.get_barrier_semaphore()
    pl.semaphore_signal(barrier, inc=1, device_id={"row": partner}, device_id_type=MESH)
    pl.semaphore_signal(barrier, inc=1, device_id={"row": inward}, device_id_type=MESH)

    @pl.when(jnp.logical_not(is_end))
    def _():
        pl.semaphore_signal(barrier, inc=1, device_id={"row": outward}, device_id_type=MESH)

    pl.semaphore_wait(barrier, jnp.where(is_end, 2, 3))

    up = STRIDE
    root = up + half * STRIDE
    cross = root + STRIDE
    total = root + STRIDE
    total2 = cross + STRIDE
    last = total2 + (half - 1) * STRIDE

    block = 32
    per = 8
    pieces = rank // per
    begin = last + 2 * STRIDE + first

    def eliminate(t):
        k0 = (t * per // block) * block
        part = t % (block // per)
        tile = (k0 // LANES) * LANES
        shift = k0 % LANES
        r = lax.broadcasted_iota(jnp.int32, (block, LANES), 0)
        l = lax.broadcasted_iota(jnp.int32, (block, LANES), 1)
        if part == 0:
            d = factor[k0 : k0 + block, tile : tile + LANES]
            if shift:
                d = pltpu.roll(d, LANES - shift, 1)
            aug = jnp.where(l < block, d, jnp.where(l - block == r, 1.0, 0.0))
        else:
            aug = panel[...]
        for j in range(part * per, (part + 1) * per):
            column = jnp.broadcast_to(aug[:, j : j + 1], (block, LANES))
            pivot = column[j : j + 1, :]
            ratio = jnp.where(r > j, column * (1.0 / pivot), 0.0)
            aug = aug - ratio * aug[j : j + 1, :]
        if part < block // per - 1:
            panel[...] = aug
            return
        diagonal = jnp.sum(jnp.where(l == r, aug, 0.0), axis=1, keepdims=True)
        t_inv = (aug * lax.rsqrt(diagonal))[:, block : 2 * block]
        rw = lax.broadcasted_iota(jnp.int32, (block, rank), 0)
        lw = lax.broadcasted_iota(jnp.int32, (block, rank), 1)
        inside = (lw >= k0) & (lw < k0 + block)
        own = jnp.where(inside, jnp.where(lw - k0 == rw, 1.0, 0.0), factor[k0 : k0 + block, :])
        done = matmul(t_inv, own, ((1,), (0,)), HIGHEST)
        factor[k0 : k0 + block, :] = done
        rest = rank - k0 - block
        if rest:
            below = factor[k0 + block :, :]
            left_part = matmul(below[:, k0 : k0 + block], t_inv, ((1,), (1,)), HIGHEST)
            lb = lax.broadcasted_iota(jnp.int32, (rest, rank), 1)
            kept = jnp.where((lb >= k0) & (lb < k0 + block), 0.0, below)
            factor[k0 + block :, :] = kept - matmul(left_part, done, ((1,), (0,)), HIGHEST)

    @pl.loop(0, chunks + last + STRIDE)
    def _(i):
        @pl.when(i < chunks)
        def _():
            c = i

            @pl.when(c >= first)
            def _():
                j = c - first
                slot = lax.rem(j, 2)

                @pl.when(j + 1 < chunks - first)
                def _():
                    for copy in load(j + 1, 1 - slot):
                        copy.start()

                for copy in load(j, slot):
                    copy.wait()
                b_high, b_low = split(states[slot] + slopes[slot].astype(jnp.float32))
                dims = ((1,), (0,))
                work[c] = (
                    matmul(turned[0], b_high, dims, None)
                    + matmul(turned[0], b_low, dims, None)
                    + matmul(turned[1], b_high, dims, None)
                )

            copies[0](c).start()

        def stage(offset, action, when=True):
            c = i - offset

            @pl.when((c >= 0) & (c < chunks) & when)
            def _():
                action(c)

        def upward(c):
            copies[0](c).wait_recv()
            add(work, c, mine, pair, 0, 2 * size)

            @pl.when(jnp.logical_not(is_end))
            def _():
                copies[1](c).wait_recv()
                copies[2](c).wait_recv()
                add(work, c, mine, outer, 0, 2 * size)
                add(work, c, 4 * size, outer, 2 * size, 4 * size)

            @pl.when(is_middle)
            def _():
                copies[3](c).start()
                copies[4](c).start()

            @pl.when(jnp.logical_not(is_middle))
            def _():
                copies[1](c).start()
                copies[2](c).start()

        def rooted(c):
            copies[3](c).wait_recv()
            add(fin, c, near1, middle, 0, size)
            copies[6](c).start()
            copies[4](c).wait_recv()
            add(work, c, near2, middle, size, 2 * size)
            copies[5](c).start()

        def crossed(c):
            copies[5](c).wait_recv()
            add(fin, c, near2, pair, 2 * size, 2 * size)
            copies[7](c).start()

        def totals(c, kind, out, pairwise):
            @pl.when(is_middle)
            def _():
                copies[kind](c).wait_recv()

            @pl.when(jnp.logical_not(is_middle))
            def _():
                copies[out](c).wait_recv()

            @pl.when(jnp.logical_not(is_end))
            def _():
                copies[out](c).start()

            if pairwise:
                copies[10](c).start()

        stage(up + depth * STRIDE, upward)
        stage(root, rooted, is_middle)
        stage(cross, crossed, is_middle)
        away = (half - 1 - depth) * STRIDE
        stage(total + away, lambda c: totals(c, 6, 8, True))
        stage(total2 + away, lambda c: totals(c, 7, 9, False))
        stage(last + STRIDE - 1, lambda c: copies[10](c).wait_recv())

        for t in range(pieces):
            @pl.when(i == begin + t)
            def _():
                if t == 0:
                    gram = jnp.concatenate([fin[k] for k in range(first)], axis=1)
                    factor[...] = 0.5 * (gram + gram.T)
                eliminate(t)

    for t in range(pieces):
        @pl.when(chunks + last + STRIDE <= begin + t)
        def _():
            if t == 0:
                gram = jnp.concatenate([fin[k] for k in range(first)], axis=1)
                factor[...] = 0.5 * (gram + gram.T)
            eliminate(t)

    r = lax.broadcasted_iota(jnp.int32, (rank, rank), 0)
    l = lax.broadcasted_iota(jnp.int32, (rank, rank), 1)
    inverse[...] = jnp.where(l <= r, factor[...], 0.0)

    @pl.loop(0, chunks)
    def _(c):
        copies[0](c).wait_send()
        copies[10](c).wait_send()

        @pl.when(is_middle)
        def _():
            for kind in (3, 4, 5, 6, 7):
                copies[kind](c).wait_send()

        @pl.when(jnp.logical_not(is_middle))
        def _():
            copies[1](c).wait_send()
            copies[2](c).wait_send()

        @pl.when(jnp.logical_not(is_end))
        def _():
            copies[8](c).wait_send()
            copies[9](c).wait_send()


def row_reduce(state, grads, step, projected, row_size, collective_id):
    rows, columns = state.shape
    rank = projected.shape[1]
    chunks = (columns + rank) // LANES
    vmem = pl.BlockSpec(memory_space=pltpu.VMEM)
    hbm = pl.BlockSpec(memory_space=pl.ANY)
    size = rank // 8
    f32 = jnp.float32
    fin, inverse = pl.pallas_call(
        functools.partial(row_kernel, row_size, step),
        out_shape=[
            jax.ShapeDtypeStruct((chunks, rank, LANES), f32),
            jax.ShapeDtypeStruct((rank, rank), f32),
        ],
        in_specs=[hbm, hbm, vmem],
        out_specs=[vmem, vmem],
        scratch_shapes=[
            pltpu.VMEM((chunks, rank, LANES), f32),
            pltpu.VMEM((chunks, 6 * size, LANES), f32),
            pltpu.VMEM((chunks, 3 * size, LANES), f32),
            pltpu.VMEM((chunks, 4 * size, LANES), f32),
            pltpu.VMEM((2, rank, rows), jnp.bfloat16),
            pltpu.VMEM((rank, rank), f32),
            pltpu.VMEM((32, LANES), f32),
            pltpu.VMEM((2, rows, LANES), f32),
            pltpu.VMEM((2, rows, LANES), jnp.bfloat16),
            pltpu.SemaphoreType.DMA((2, 2)),
            pltpu.SemaphoreType.DMA((KINDS, chunks)),
            pltpu.SemaphoreType.DMA((KINDS, chunks)),
        ],
        compiler_params=pltpu.CompilerParams(
            collective_id=collective_id, has_side_effects=True, vmem_limit_bytes=40 * 2**20
        ),
        cost_estimate=pl.CostEstimate(
            flops=6 * rows * columns * rank, bytes_accessed=6 * rows * columns, transcendentals=0
        ),
    )(state, grads, projected)
    return fin[rank // LANES :], inverse


def shards(row_size, col_size, momentum, grads, basis):
    rank = basis.shape[1]
    factor = (momentum.shape[0] * row_size * momentum.shape[1] * col_size / rank) ** 0.5
    state = momentum
    right = basis
    scale = None
    squares = None
    left = None
    change = 0.0
    steps = grads.shape[0]
    for step in range(steps):
        buffer = state + grads[step].astype(jnp.float32)
        partial_value = matmul(buffer, right, ((1,), (0,)), HIGH)
        if step == 0:
            (projected,) = all_reduce([partial_value], "col", col_size, 0)
        else:
            projected, squares = all_reduce([partial_value, squares], "col", col_size, 1)
            scale = lax.rsqrt(squares[:1] + norm_eps)
            projected = projected * scale
            change = change + factor * matmul(left, right * scale, ((1,), (1,)), HIGH)
        product, inverse = row_reduce(state, grads, step, projected, row_size, 2 + step)
        ortho = matmul(projected, inverse, ((1,), (1,)), HIGHEST)
        raw = matmul(product, inverse, ((1,), (1,)), HIGH).reshape(-1, rank)
        left = ortho
        squares = jnp.pad(jnp.sum(raw * raw, axis=0, keepdims=True), ((0, 8 * col_size - 1), (0, 0)))
        right = raw
        state = buffer - (1.0 - keep_rate) * matmul(
            ortho.astype(jnp.bfloat16), raw.astype(jnp.bfloat16), ((1,), (1,)), None
        )
    (squares,) = all_reduce([squares], "col", col_size, 4)
    scale = lax.rsqrt(squares[:1] + norm_eps)
    change = change + factor * matmul(left, right * scale, ((1,), (1,)), HIGH)
    return (change.astype(jnp.bfloat16), state)


def solution(mesh):
    return jax.shard_map(
        functools.partial(shards, mesh.shape["row"], mesh.shape["col"]),
        mesh=mesh,
        in_specs=(P("row", "col"), P(None, "row", "col"), P("col", None)),
        out_specs=(P("row", "col"), P("row", "col")),
        check_vma=False,
    )
```

```python
import functools

import jax
import jax.numpy as jnp
from jax import lax
from jax.experimental import pallas as pl
from jax.experimental.pallas import tpu as pltpu
from jax.sharding import PartitionSpec as P

keep_rate = 0.95
norm_eps = 1e-06
HIGH = lax.Precision.HIGH
HIGHEST = lax.Precision.HIGHEST
MESH = pl.DeviceIdType.MESH
LANES = 128
STRIDE = 2
SLOTS = 3
WIDTH = 256


def matmul(a, b, dims, precision):
    return lax.dot_general(a, b, (dims, ((), ())), precision=precision, preferred_element_type=jnp.float32)


def split(x):
    high = x.astype(jnp.bfloat16)
    return high, (x - high.astype(jnp.float32)).astype(jnp.bfloat16)


KINDS = 12


def row_kernel(rows, cols, step, *refs):
    state, refs = refs[0], refs[1:]
    if step is not None:
        grads, refs = refs[0], refs[1:]
    projected, ortho, raw, scale, refs = *refs[:4], refs[4:]
    fin, work, upward, pair, turned, factor, panel, squares, slots, states, refs = *refs[:10], refs[10:]
    if step is not None:
        slopes, refs = refs[0], refs[1:]
    load_sem, send_sem, recv_sem, norm_send, norm_recv = refs
    line = rows // 2
    rank = factor.shape[0]
    first = rank // WIDTH
    chunks = fin.shape[0]
    size = rank // 8
    me = lax.axis_index("row")
    y = lax.rem(me, 2)
    z = me // 2
    partner = me + 1 - 2 * y
    mine = pl.multiple_of(2 * size * y, 8)
    yours = pl.multiple_of(2 * size * (1 - y), 8)
    away = (z, line - 1 - z)
    nearer = (me - 2, me + 2)
    farther = (me + 2, me - 2)
    one = tuple(pl.multiple_of(mine + size * p, 8) for p in range(2))
    two = tuple(4 * size + 2 * size * p for p in range(2))

    def load(j, slot):
        columns = pl.ds(pl.multiple_of(j * WIDTH, WIDTH), WIDTH)
        copies = [pltpu.make_async_copy(state.at[:, columns], states.at[slot], load_sem.at[0, slot])]
        if step is not None:
            copies.append(pltpu.make_async_copy(grads.at[step, :, columns], slopes.at[slot], load_sem.at[1, slot]))
        return copies

    for j in range(SLOTS - 1):
        for copy in load(j, j):
            copy.start()

    def send(kind, c, source, start, target, at, count, device):
        return pltpu.make_async_remote_copy(
            src_ref=source.at[c, pl.ds(start, count)],
            dst_ref=target.at[c, pl.ds(at, count)],
            send_sem=send_sem.at[kind, c],
            recv_sem=recv_sem.at[kind, c],
            device_id={"row": device},
            device_id_type=MESH,
        )

    copies = {0: lambda c: send(0, c, work, yours, pair, 0, 2 * size, partner)}
    for p in range(2):
        n, f, o, t = nearer[p], farther[p], one[p], two[p]
        up = upward.at[p]
        copies[1 + p] = functools.partial(send, 1 + p, source=work, start=o, target=up, at=0, count=size, device=n)
        copies[3 + p] = functools.partial(
            send, 3 + p, source=work, start=t, target=up, at=size, count=2 * size, device=n
        )
        copies[6 + p] = functools.partial(send, 6 + p, source=fin, start=o, target=fin, at=o, count=size, device=f)
        copies[8 + p] = functools.partial(send, 8 + p, source=fin, start=t, target=fin, at=t, count=2 * size, device=f)
        copies[10 + p] = functools.partial(
            send, 10 + p, source=fin, start=o, target=fin, at=o, count=size, device=partner
        )
    cross = [
        functools.partial(
            send, 5, source=work, start=two[p], target=pair, at=2 * size, count=2 * size, device=partner
        )
        for p in range(2)
    ]

    def add(target, c, start, source, at, count):
        target[c, pl.ds(start, count), :] = work[c, pl.ds(start, count), :] + source[c, pl.ds(at, count), :]

    transposed = projected[...].T
    high, low = split(transposed)
    turned[0] = high
    turned[1] = low
    gram = matmul(transposed, transposed, ((1,), (1,)), HIGHEST)
    for k in range(first):
        work[k] = gram[:, k * WIDTH : (k + 1) * WIDTH]

    barrier = pltpu.get_barrier_semaphore()
    pl.semaphore_signal(barrier, inc=1, device_id={"row": partner}, device_id_type=MESH)
    for p in range(2):
        @pl.when(away[p] > 0)
        def _():
            pl.semaphore_signal(barrier, inc=1, device_id={"row": nearer[p]}, device_id_type=MESH)

    mine_col = lax.axis_index("col")
    others = [lax.rem(mine_col + d, cols) for d in range(1, cols)]
    for other in others:
        pl.semaphore_signal(barrier, inc=1, device_id={"col": other}, device_id_type=MESH)
    pl.semaphore_wait(barrier, jnp.where((z == 0) | (z == line - 1), 2, 3) + cols - 1)

    turn = line * STRIDE
    delay = max(turn, chunks + 1 - 2 * STRIDE) - turn
    last = 2 * turn + delay

    block = 32
    per = 16
    pieces = rank // per
    begin = 2 * turn + first

    def eliminate(t):
        k0 = (t * per // block) * block
        part = t % (block // per)
        tile = (k0 // LANES) * LANES
        shift = k0 % LANES
        r = lax.broadcasted_iota(jnp.int32, (block, LANES), 0)
        l = lax.broadcasted_iota(jnp.int32, (block, LANES), 1)
        if part == 0:
            d = factor[k0 : k0 + block, tile : tile + LANES]
            if shift:
                d = pltpu.roll(d, LANES - shift, 1)
            aug = jnp.where(l < block, d, jnp.where(l - block == r, 1.0, 0.0))
        else:
            aug = panel[...]
        for j in range(part * per, (part + 1) * per):
            column = jnp.broadcast_to(aug[:, j : j + 1], (block, LANES))
            pivot = column[j : j + 1, :]
            ratio = jnp.where(r > j, column * (1.0 / pivot), 0.0)
            aug = aug - ratio * aug[j : j + 1, :]
        if part < block // per - 1:
            panel[...] = aug
            return
        diagonal = jnp.sum(jnp.where(l == r, aug, 0.0), axis=1, keepdims=True)
        t_inv = (aug * lax.rsqrt(diagonal))[:, block : 2 * block]
        rw = lax.broadcasted_iota(jnp.int32, (block, rank), 0)
        lw = lax.broadcasted_iota(jnp.int32, (block, rank), 1)
        inside = (lw >= k0) & (lw < k0 + block)
        own = jnp.where(inside, jnp.where(lw - k0 == rw, 1.0, 0.0), factor[k0 : k0 + block, :])
        done = matmul(t_inv, own, ((1,), (0,)), HIGHEST)
        factor[k0 : k0 + block, :] = done
        rest = rank - k0 - block
        if rest:
            below = factor[k0 + block :, :]
            left_part = matmul(below[:, k0 : k0 + block], t_inv, ((1,), (1,)), HIGHEST)
            lb = lax.broadcasted_iota(jnp.int32, (rest, rank), 1)
            kept = jnp.where((lb >= k0) & (lb < k0 + block), 0.0, below)
            factor[k0 + block :, :] = kept - matmul(left_part, done, ((1,), (0,)), HIGHEST)

    def finish():
        r = lax.broadcasted_iota(jnp.int32, (rank, rank), 0)
        l = lax.broadcasted_iota(jnp.int32, (rank, rank), 1)
        inverse = jnp.where(l <= r, factor[...], 0.0)
        high, low = split(inverse)
        turned[0, :, :rank] = high
        turned[1, :, :rank] = low
        ortho[...] = matmul(projected[...], inverse, ((1,), (1,)), HIGHEST)
        squares[...] = jnp.zeros_like(squares)

    def expand(c):
        t_high, t_low = split(fin[c])
        i_high, i_low = turned[0, :, :rank], turned[1, :, :rank]
        dims = ((1,), (0,))
        value = matmul(i_high, t_high, dims, None) + matmul(i_high, t_low, dims, None) + matmul(i_low, t_high, dims, None)
        raw[c - first] = value
        square = value * value
        squares[...] += sum(square[:, k : k + LANES] for k in range(0, WIDTH, LANES))

    total = chunks + last
    ready = max(begin + pieces, chunks)

    def reached(i):
        count = jnp.minimum(jnp.minimum(first + 3 * (i - ready + 1), i - (last - 1) + 1), chunks)
        return jnp.maximum(count, first)

    @pl.loop(0, total)
    def _(i):
        @pl.when(i < chunks)
        def _():
            c = i

            @pl.when(c >= first)
            def _():
                j = c - first
                slot = lax.rem(j, SLOTS)
                ahead = j + SLOTS - 1

                @pl.when(ahead < chunks - first)
                def _():
                    for copy in load(ahead, lax.rem(ahead, SLOTS)):
                        copy.start()

                for copy in load(j, slot):
                    copy.wait()
                buffer = states[slot]
                if step is not None:
                    buffer = buffer + slopes[slot].astype(jnp.float32)
                b_high, b_low = split(buffer)
                dims = ((1,), (0,))
                work[c] = (
                    matmul(turned[0], b_high, dims, None)
                    + matmul(turned[0], b_low, dims, None)
                    + matmul(turned[1], b_high, dims, None)
                )

            copies[0](c).start()

        def stage(offset, action, when=True, low=0, high=chunks):
            c = i - offset

            @pl.when((c >= low) & (c < high) & when)
            def _():
                action(c)

        def paired(c):
            copies[0](c).wait_recv()
            add(work, c, mine, pair, 0, 2 * size)

        def rise_one(c, p):
            @pl.when(away[p] < line - 1)
            def _():
                copies[1 + p](c).wait_recv()

                @pl.when(away[p] > 0)
                def _():
                    add(work, c, one[p], upward.at[p], 0, size)

                @pl.when(away[p] == 0)
                def _():
                    add(fin, c, one[p], upward.at[p], 0, size)

            @pl.when(away[p] > 0)
            def _():
                copies[1 + p](c).start()

        def rise_two(c, p):
            @pl.when(away[p] < line - 1)
            def _():
                copies[3 + p](c).wait_recv()
                add(work, c, two[p], upward.at[p], size, 2 * size)

            @pl.when(away[p] > 0)
            def _():
                copies[3 + p](c).start()

        def exchange(c, p):
            cross[p](c).start()

        def crossed(c, p):
            cross[p](c).wait_recv()
            add(fin, c, two[p], pair, 2 * size, 2 * size)

        def fall(c, p):
            @pl.when(away[p] > 0)
            def _():
                copies[6 + p](c).wait_recv()

            @pl.when(away[p] < line - 1)
            def _():
                copies[6 + p](c).start()

            copies[10 + p](c).start()

            @pl.when(away[p] > 0)
            def _():
                copies[8 + p](c).wait_recv()

            @pl.when(away[p] < line - 1)
            def _():
                copies[8 + p](c).start()

        def gathered(c):
            copies[10](c).wait_recv()
            copies[11](c).wait_recv()

        stage(STRIDE, paired)
        for p in range(2):
            height = (line - 1 - away[p]) * STRIDE
            stage(height, functools.partial(rise_two, p=p))
            stage(STRIDE + height, functools.partial(rise_one, p=p))
        for low, high, later in ((0, first, 0), (first, chunks, delay)):
            for p in range(2):
                at = turn - STRIDE + later // 2
                stage(at, functools.partial(exchange, p=p), away[p] == 0, low, high)
                stage(at + STRIDE, functools.partial(crossed, p=p), away[p] == 0, low, high)
                stage(turn + later + away[p] * STRIDE, functools.partial(fall, p=p), True, low, high)
            stage(2 * turn + later - 1, gathered, True, low, high)

        for t in range(pieces):
            @pl.when(i == begin + t)
            def _():
                if t == 0:
                    gram = jnp.concatenate([fin[k] for k in range(first)], axis=1)
                    factor[...] = 0.5 * (gram + gram.T)
                eliminate(t)

        if ready < total:
            @pl.when(i == ready)
            def _():
                finish()

            @pl.when(i >= ready)
            def _():
                @pl.loop(reached(i - 1), reached(i))
                def _(c):
                    expand(c)

    for t in range(pieces):
        if total <= begin + t:
            if t == 0:
                gram = jnp.concatenate([fin[k] for k in range(first)], axis=1)
                factor[...] = 0.5 * (gram + gram.T)
            eliminate(t)
    if total <= ready:
        finish()

    done = min(max(first + 3 * (total - ready), first), chunks) if ready < total else first

    @pl.loop(done, chunks)
    def _(c):
        expand(c)

    slots[mine_col] = matmul(jnp.ones((8, LANES), jnp.float32), squares[...], ((1,), (1,)), HIGHEST)
    norms = [
        pltpu.make_async_remote_copy(
            src_ref=slots.at[mine_col],
            dst_ref=slots.at[mine_col],
            send_sem=norm_send.at[d],
            recv_sem=norm_recv.at[d],
            device_id={"col": other},
            device_id_type=MESH,
        )
        for d, other in enumerate(others)
    ]
    for copy in norms:
        copy.start()

    @pl.loop(0, chunks)
    def _(c):
        for kind in (0, 10, 11):
            copies[kind](c).wait_send()
        for p in range(2):
            @pl.when(away[p] > 0)
            def _():
                copies[1 + p](c).wait_send()
                copies[3 + p](c).wait_send()

            @pl.when(away[p] == 0)
            def _():
                cross[p](c).wait_send()

            @pl.when(away[p] < line - 1)
            def _():
                copies[6 + p](c).wait_send()
                copies[8 + p](c).wait_send()

    for copy in norms:
        copy.wait()
    whole = slots[0]
    for d in range(1, cols):
        whole = whole + slots[d]
    scale[...] = lax.rsqrt(whole + norm_eps)


def row_reduce(state, grads, step, projected, row_size, col_size, collective_id):
    rows, columns = state.shape
    rank = projected.shape[1]
    chunks = (columns + rank) // WIDTH
    vmem = pl.BlockSpec(memory_space=pltpu.VMEM)
    hbm = pl.BlockSpec(memory_space=pl.ANY)
    size = rank // 8
    f32 = jnp.float32
    operands = (state, projected) if step is None else (state, grads, projected)
    return pl.pallas_call(
        functools.partial(row_kernel, row_size, col_size, step),
        out_shape=[
            jax.ShapeDtypeStruct((rows, rank), f32),
            jax.ShapeDtypeStruct((columns // WIDTH, rank, WIDTH), f32),
            jax.ShapeDtypeStruct((8, rank), f32),
        ],
        in_specs=[hbm] * (len(operands) - 1) + [vmem],
        out_specs=[vmem] * 3,
        scratch_shapes=[
            pltpu.VMEM((chunks, rank, WIDTH), f32),
            pltpu.VMEM((chunks, rank, WIDTH), f32),
            pltpu.VMEM((2, chunks, 3 * size, WIDTH), f32),
            pltpu.VMEM((chunks, 4 * size, WIDTH), f32),
            pltpu.VMEM((2, rank, rows), jnp.bfloat16),
            pltpu.VMEM((rank, rank), f32),
            pltpu.VMEM((32, LANES), f32),
            pltpu.VMEM((rank, LANES), f32),
            pltpu.VMEM((col_size, 8, rank), f32),
            pltpu.VMEM((SLOTS, rows, WIDTH), f32),
        ]
        + ([] if step is None else [pltpu.VMEM((SLOTS, rows, WIDTH), jnp.bfloat16)])
        + [
            pltpu.SemaphoreType.DMA((2, SLOTS)),
            pltpu.SemaphoreType.DMA((KINDS, chunks)),
            pltpu.SemaphoreType.DMA((KINDS, chunks)),
            pltpu.SemaphoreType.DMA((col_size - 1,)),
            pltpu.SemaphoreType.DMA((col_size - 1,)),
        ],
        compiler_params=pltpu.CompilerParams(
            collective_id=collective_id, has_side_effects=True, vmem_limit_bytes=46 * 2**20
        ),
        cost_estimate=pl.CostEstimate(
            flops=6 * rows * columns * rank, bytes_accessed=6 * rows * columns, transcendentals=0
        ),
    )(*operands)


def project_kernel(cols, step, *refs):
    state, grads, right, refs = *refs[:3], refs[3:]
    if step:
        ortho, scale, refs = *refs[:2], refs[2:]
    projected, refs = refs[0], refs[1:]
    if step:
        buffer, refs = refs[0], refs[1:]
    states, slopes, high, low, part, pair, sums, recvs, refs = *refs[:8], refs[8:]
    if step:
        buffers, left, store_sem, refs = *refs[:3], refs[3:]
    load_sem, send_sem, recv_sem = refs
    tall = states.shape[1]
    rows, rank = projected.shape
    columns = state.shape[1]
    blocks = rows // tall
    half = tall // 2
    bits = cols.bit_length() - 1
    me = lax.axis_index("col")
    partners = [me + (1 - 2 * lax.rem(me // (1 << b), 2)) * (1 << b) for b in range(bits)]
    mine = pl.multiple_of(half * lax.rem(me, 2), 8)
    yours = pl.multiple_of(half * (1 - lax.rem(me, 2)), 8)

    def load(r):
        where = pl.ds(r * tall, tall)
        slot = r % 2
        copies = [pltpu.make_async_copy(state.at[where], states.at[slot], load_sem.at[0, slot])]
        for g in range(step + 1):
            copies.append(
                pltpu.make_async_copy(grads.at[g, where], slopes.at[slot, g], load_sem.at[1 + g, slot])
            )
        return copies

    for copy in load(0):
        copy.start()

    barrier = pltpu.get_barrier_semaphore()
    for partner in partners:
        pl.semaphore_signal(barrier, inc=1, device_id={"col": partner}, device_id_type=MESH)

    if step:
        for c in range(columns // WIDTH):
            at = slice(c * WIDTH, (c + 1) * WIDTH)
            high[:, at], low[:, at] = split(right[c])
        left[...] = ortho[...].astype(jnp.bfloat16)
    else:
        high[...], low[...] = split(right[...])

    pl.semaphore_wait(barrier, bits)

    def remote(kind, r, source, target, partner):
        return pltpu.make_async_remote_copy(
            src_ref=source,
            dst_ref=target,
            send_sem=send_sem.at[kind, r],
            recv_sem=recv_sem.at[kind, r],
            device_id={"col": partner},
            device_id_type=MESH,
        )

    def swap(r):
        return remote(0, r, part.at[r, pl.ds(yours, half)], pair.at[r], partners[0])

    def cross(b, r):
        return remote(b, r, sums.at[b - 1, r], recvs.at[b - 1, r], partners[b])

    def whole(r):
        return projected.at[pl.ds(pl.multiple_of(r * tall + mine, 8), half)]

    def gather(r):
        return remote(bits, r, whole(r), whole(r), partners[0])

    def arrive(k, r):
        if k == bits + 1:
            gather(r).wait_recv()
            return
        if k == 1:
            swap(r).wait_recv()
            value = part[r, pl.ds(mine, half), :] + pair[r]
        else:
            cross(k - 1, r).wait_recv()
            value = sums[k - 2, r] + recvs[k - 2, r]
        if k < bits:
            sums[k - 1, r] = value
            cross(k, r).start()
        else:
            if step:
                value = value * scale[0:1, :]
            whole(r)[...] = value
            gather(r).start()

    deep = min(columns, 1024)
    for t in range(blocks + bits + 1):
        if t < blocks:
            slot = t % 2
            if t + 1 < blocks:
                for copy in load(t + 1):
                    copy.start()
            for copy in load(t):
                copy.wait()
            if step and t >= 2:
                store(t - 2).wait()
            part[t] = jnp.zeros(part.shape[1:], jnp.float32)

            @pl.loop(0, columns // deep)
            def _(k):
                at = pl.ds(pl.multiple_of(k * deep, deep), deep)
                value = states[slot, :, at] + slopes[slot, 0, :, at].astype(jnp.float32)
                if step:
                    update = matmul(left[t * tall : (t + 1) * tall, :], high[:, at], ((1,), (0,)), None)
                    value = value - (1.0 - keep_rate) * update
                    value = value + slopes[slot, 1, :, at].astype(jnp.float32)
                    buffers[slot, :, at] = value
                    r_high, r_low, dims = high[:, at], low[:, at], ((1,), (1,))
                else:
                    r_high, r_low, dims = high[at, :], low[at, :], ((1,), (0,))
                v_high, v_low = split(value)
                part[t] += (
                    matmul(v_high, r_high, dims, None)
                    + matmul(v_low, r_high, dims, None)
                    + matmul(v_high, r_low, dims, None)
                )

            if step:
                def store(r):
                    return pltpu.make_async_copy(
                        buffers.at[r % 2], buffer.at[pl.ds(r * tall, tall)], store_sem.at[r % 2]
                    )

                store(t).start()
            swap(t).start()
        for r in range(blocks):
            if 1 <= t - r <= bits + 1:
                arrive(t - r, r)

    for r in range(blocks):
        swap(r).wait_send()
        gather(r).wait_send()
        for b in range(1, bits):
            cross(b, r).wait_send()
        if step and r >= blocks - 2:
            store(r).wait()


def project(state, grads, step, right, ortho, scale, col_size, collective_id):
    rows, columns = state.shape
    rank = right.shape[1]
    tall = min(256, rows)
    blocks = rows // tall
    bits = col_size.bit_length() - 1
    vmem = pl.BlockSpec(memory_space=pltpu.VMEM)
    hbm = pl.BlockSpec(memory_space=pl.ANY)
    f32, bf16 = jnp.float32, jnp.bfloat16
    operands = (state, grads, right) + ((ortho, scale) if step else ())
    shape = (rank, columns) if step else (columns, rank)
    out_shape = [jax.ShapeDtypeStruct((rows, rank), f32)]
    scratch = [
        pltpu.VMEM((2, tall, columns), f32),
        pltpu.VMEM((2, step + 1, tall, columns), bf16),
        pltpu.VMEM(shape, bf16),
        pltpu.VMEM(shape, bf16),
        pltpu.VMEM((blocks, tall, rank), f32),
        pltpu.VMEM((blocks, tall // 2, rank), f32),
        pltpu.VMEM((bits - 1, blocks, tall // 2, rank), f32),
        pltpu.VMEM((bits - 1, blocks, tall // 2, rank), f32),
    ]
    if step:
        out_shape.append(jax.ShapeDtypeStruct((rows, columns), f32))
        scratch += [
            pltpu.VMEM((2, tall, columns), f32),
            pltpu.VMEM((rows, rank), bf16),
            pltpu.SemaphoreType.DMA((2,)),
        ]
    return pl.pallas_call(
        functools.partial(project_kernel, col_size, step),
        out_shape=out_shape,
        in_specs=[hbm, hbm] + [vmem] * (len(operands) - 2),
        out_specs=[vmem, hbm][: step + 1],
        scratch_shapes=scratch
        + [
            pltpu.SemaphoreType.DMA((2 + step, 2)),
            pltpu.SemaphoreType.DMA((bits + 1, blocks)),
            pltpu.SemaphoreType.DMA((bits + 1, blocks)),
        ],
        compiler_params=pltpu.CompilerParams(
            collective_id=collective_id, has_side_effects=True, vmem_limit_bytes=52 * 2**20
        ),
        cost_estimate=pl.CostEstimate(
            flops=8 * rows * columns * rank, bytes_accessed=10 * rows * columns, transcendentals=0
        ),
    )(*operands)


def finish_kernel(gain, buffer, ortho, raw, scale, left, right, before, change, state, lefts, highs):
    @pl.when(pl.program_id(0) == 0)
    def _():
        lefts[0, 0], lefts[0, 1] = split(left[...] * (before[0:1, :] * gain))
        lefts[1, 0], lefts[1, 1] = split(ortho[...] * (scale[0:1, :] * gain))
        highs[...] = ortho[...].astype(jnp.bfloat16)

    dims = ((1,), (0,))
    r_high, r_low = split(raw[0])
    state[...] = buffer[...] - (1.0 - keep_rate) * matmul(highs[...], r_high, dims, None)
    p_high, p_low = split(right[0])
    total = matmul(lefts[0, 0], p_high, dims, None)
    total = total + matmul(lefts[0, 1], p_high, dims, None)
    total = total + matmul(lefts[0, 0], p_low, dims, None)
    total = total + matmul(lefts[1, 0], r_high, dims, None)
    total = total + matmul(lefts[1, 1], r_high, dims, None)
    total = total + matmul(lefts[1, 0], r_low, dims, None)
    change[...] = total.astype(jnp.bfloat16)


def finish(gain, buffer, ortho, raw, scale, left, right, before):
    rows, columns = buffer.shape
    rank = ortho.shape[1]
    tile = pl.BlockSpec((rows, WIDTH), lambda c: (0, c))
    chunk = pl.BlockSpec((1, rank, WIDTH), lambda c: (c, 0, 0))
    tall = pl.BlockSpec((rows, rank), lambda c: (0, 0))
    row = pl.BlockSpec((8, rank), lambda c: (0, 0))
    return pl.pallas_call(
        functools.partial(finish_kernel, gain),
        grid=(columns // WIDTH,),
        out_shape=[
            jax.ShapeDtypeStruct((rows, columns), jnp.bfloat16),
            jax.ShapeDtypeStruct((rows, columns), jnp.float32),
        ],
        in_specs=[tile, tall, chunk, row, tall, chunk, row],
        out_specs=[tile, tile],
        scratch_shapes=[
            pltpu.VMEM((2, 2, rows, rank), jnp.bfloat16),
            pltpu.VMEM((rows, rank), jnp.bfloat16),
        ],
        compiler_params=pltpu.CompilerParams(vmem_limit_bytes=40 * 2**20),
        cost_estimate=pl.CostEstimate(
            flops=14 * rows * columns * rank, bytes_accessed=10 * rows * columns, transcendentals=0
        ),
    )(buffer, ortho, raw, scale, left, right, before)


def shards(row_size, col_size, momentum, grads, basis):
    rank = basis.shape[1]
    gain = (momentum.shape[0] * row_size * momentum.shape[1] * col_size / rank) ** 0.5
    (projected,) = project(momentum, grads, 0, basis, None, None, col_size, 0)
    left, right, before = row_reduce(momentum, grads, 0, projected, row_size, col_size, 1)
    projected, buffer = project(momentum, grads, 1, right, left, before, col_size, 2)
    ortho, raw, scale = row_reduce(buffer, None, None, projected, row_size, col_size, 3)
    return tuple(finish(gain, buffer, ortho, raw, scale, left, right, before))


def solution(mesh):
    return jax.shard_map(
        functools.partial(shards, mesh.shape["row"], mesh.shape["col"]),
        mesh=mesh,
        in_specs=(P("row", "col"), P(None, "row", "col"), P("col", None)),
        out_specs=(P("row", "col"), P("row", "col")),
        check_vma=False,
    )
```

```python
import functools

import jax
import jax.numpy as jnp
from jax import lax
from jax.experimental import pallas as pl
from jax.experimental.pallas import tpu as pltpu
from jax.sharding import PartitionSpec as P

keep_rate = 0.95
norm_eps = 1e-06
HIGH = lax.Precision.HIGH
HIGHEST = lax.Precision.HIGHEST
MESH = pl.DeviceIdType.MESH
LANES = 128
STRIDE = 2
SLOTS = 3
WIDTH = 256
LAG = 3


def matmul(a, b, dims, precision):
    return lax.dot_general(a, b, (dims, ((), ())), precision=precision, preferred_element_type=jnp.float32)


def split(x):
    high = x.astype(jnp.bfloat16)
    return high, (x - high.astype(jnp.float32)).astype(jnp.bfloat16)


KINDS = 12


def row_kernel(rows, cols, step, *refs):
    state, refs = refs[0], refs[1:]
    if step is not None:
        grads, refs = refs[0], refs[1:]
    projected, ortho, raw, scale, refs = *refs[:4], refs[4:]
    fin, work, upward, pair, turned, factor, panel, squares, slots, states, refs = *refs[:10], refs[10:]
    if step is not None:
        slopes, refs = refs[0], refs[1:]
    ortho_here, raw_here, load_sem, send_sem, recv_sem, norm_send, norm_recv, out_sem = refs
    line = rows // 2
    rank = factor.shape[0]
    first = rank // WIDTH
    chunks = fin.shape[0]
    size = rank // 8
    me = lax.axis_index("row")
    y = lax.rem(me, 2)
    z = me // 2
    partner = me + 1 - 2 * y
    mine = pl.multiple_of(2 * size * y, 8)
    yours = pl.multiple_of(2 * size * (1 - y), 8)
    away = (z, line - 1 - z)
    nearer = (me - 2, me + 2)
    farther = (me + 2, me - 2)
    one = tuple(pl.multiple_of(mine + size * p, 8) for p in range(2))
    two = tuple(4 * size + 2 * size * p for p in range(2))

    def load(j, slot):
        columns = pl.ds(pl.multiple_of(j * WIDTH, WIDTH), WIDTH)
        copies = [pltpu.make_async_copy(state.at[:, columns], states.at[slot], load_sem.at[0, slot])]
        if step is not None:
            copies.append(pltpu.make_async_copy(grads.at[step, :, columns], slopes.at[slot], load_sem.at[1, slot]))
        return copies

    for j in range(SLOTS - 1):
        for copy in load(j, j):
            copy.start()

    def send(kind, c, source, start, target, at, count, device):
        return pltpu.make_async_remote_copy(
            src_ref=source.at[c, pl.ds(start, count)],
            dst_ref=target.at[c, pl.ds(at, count)],
            send_sem=send_sem.at[kind, c],
            recv_sem=recv_sem.at[kind, c],
            device_id={"row": device},
            device_id_type=MESH,
        )

    copies = {0: lambda c: send(0, c, work, yours, pair, 0, 2 * size, partner)}
    for p in range(2):
        n, f, o, t = nearer[p], farther[p], one[p], two[p]
        up = upward.at[p]
        copies[1 + p] = functools.partial(send, 1 + p, source=work, start=o, target=up, at=0, count=size, device=n)
        copies[3 + p] = functools.partial(
            send, 3 + p, source=work, start=t, target=up, at=size, count=2 * size, device=n
        )
        copies[6 + p] = functools.partial(send, 6 + p, source=fin, start=o, target=fin, at=o, count=size, device=f)
        copies[8 + p] = functools.partial(send, 8 + p, source=fin, start=t, target=fin, at=t, count=2 * size, device=f)
        copies[10 + p] = functools.partial(
            send, 10 + p, source=fin, start=o, target=fin, at=o, count=size, device=partner
        )
    cross = [
        functools.partial(
            send, 5, source=work, start=two[p], target=pair, at=2 * size, count=2 * size, device=partner
        )
        for p in range(2)
    ]

    def add(target, c, start, source, at, count):
        target[c, pl.ds(start, count), :] = work[c, pl.ds(start, count), :] + source[c, pl.ds(at, count), :]

    transposed = projected[...].T
    high, low = split(transposed)
    turned[0] = high
    turned[1] = low
    gram = matmul(transposed, transposed, ((1,), (1,)), HIGHEST)
    for k in range(first):
        work[k] = gram[:, k * WIDTH : (k + 1) * WIDTH]

    barrier = pltpu.get_barrier_semaphore()
    pl.semaphore_signal(barrier, inc=1, device_id={"row": partner}, device_id_type=MESH)
    for p in range(2):
        @pl.when(away[p] > 0)
        def _():
            pl.semaphore_signal(barrier, inc=1, device_id={"row": nearer[p]}, device_id_type=MESH)

    mine_col = lax.axis_index("col")
    others = [lax.rem(mine_col + d, cols) for d in range(1, cols)]
    for other in others:
        pl.semaphore_signal(barrier, inc=1, device_id={"col": other}, device_id_type=MESH)
    pl.semaphore_wait(barrier, jnp.where((z == 0) | (z == line - 1), 2, 3) + cols - 1)

    turn = line * STRIDE
    delay = max(turn, chunks + 1 - 2 * STRIDE) - turn
    last = 2 * turn + delay

    block = 32
    per = 16
    pieces = rank // per
    begin = 2 * turn + first

    def eliminate(t):
        k0 = (t * per // block) * block
        part = t % (block // per)
        tile = (k0 // LANES) * LANES
        shift = k0 % LANES
        r = lax.broadcasted_iota(jnp.int32, (block, LANES), 0)
        l = lax.broadcasted_iota(jnp.int32, (block, LANES), 1)
        if part == 0:
            d = factor[k0 : k0 + block, tile : tile + LANES]
            if shift:
                d = pltpu.roll(d, LANES - shift, 1)
            aug = jnp.where(l < block, d, jnp.where(l - block == r, 1.0, 0.0))
        else:
            aug = panel[...]
        for j in range(part * per, (part + 1) * per):
            column = jnp.broadcast_to(aug[:, j : j + 1], (block, LANES))
            pivot = column[j : j + 1, :]
            ratio = jnp.where(r > j, column * (1.0 / pivot), 0.0)
            aug = aug - ratio * aug[j : j + 1, :]
        if part < block // per - 1:
            panel[...] = aug
            return
        diagonal = jnp.sum(jnp.where(l == r, aug, 0.0), axis=1, keepdims=True)
        t_inv = (aug * lax.rsqrt(diagonal))[:, block : 2 * block]
        rw = lax.broadcasted_iota(jnp.int32, (block, rank), 0)
        lw = lax.broadcasted_iota(jnp.int32, (block, rank), 1)
        inside = (lw >= k0) & (lw < k0 + block)
        own = jnp.where(inside, jnp.where(lw - k0 == rw, 1.0, 0.0), factor[k0 : k0 + block, :])
        done = matmul(t_inv, own, ((1,), (0,)), HIGHEST)
        factor[k0 : k0 + block, :] = done
        rest = rank - k0 - block
        if rest:
            below = factor[k0 + block :, :]
            left_part = matmul(below[:, k0 : k0 + block], t_inv, ((1,), (1,)), HIGHEST)
            lb = lax.broadcasted_iota(jnp.int32, (rest, rank), 1)
            kept = jnp.where((lb >= k0) & (lb < k0 + block), 0.0, below)
            factor[k0 + block :, :] = kept - matmul(left_part, done, ((1,), (0,)), HIGHEST)

    def finish():
        r = lax.broadcasted_iota(jnp.int32, (rank, rank), 0)
        l = lax.broadcasted_iota(jnp.int32, (rank, rank), 1)
        inverse = jnp.where(l <= r, factor[...], 0.0)
        high, low = split(inverse)
        turned[0, :, :rank] = high
        turned[1, :, :rank] = low
        ortho_here[...] = matmul(projected[...], inverse, ((1,), (1,)), HIGHEST)
        pltpu.make_async_copy(ortho_here, ortho, out_sem.at[chunks - first]).start()
        squares[...] = jnp.zeros_like(squares)

    def expand(c):
        t_high, t_low = split(fin[c])
        i_high, i_low = turned[0, :, :rank], turned[1, :, :rank]
        dims = ((1,), (0,))
        value = matmul(i_high, t_high, dims, None) + matmul(i_high, t_low, dims, None) + matmul(i_low, t_high, dims, None)
        raw_here[c - first] = value
        pltpu.make_async_copy(raw_here.at[c - first], raw.at[c - first], out_sem.at[c - first]).start()
        square = value * value
        squares[...] += sum(square[:, k : k + LANES] for k in range(0, WIDTH, LANES))

    total = chunks + last
    ready = max(begin + pieces, chunks)

    def reached(i):
        count = jnp.minimum(jnp.minimum(first + 3 * (i - ready + 1), i - (last - 1) + 1), chunks)
        return jnp.maximum(count, first)

    @pl.loop(0, total)
    def _(i):
        @pl.when(i < chunks)
        def _():
            c = i

            @pl.when(c >= first)
            def _():
                j = c - first
                slot = lax.rem(j, SLOTS)
                ahead = j + SLOTS - 1

                @pl.when(ahead < chunks - first)
                def _():
                    for copy in load(ahead, lax.rem(ahead, SLOTS)):
                        copy.start()

                for copy in load(j, slot):
                    copy.wait()
                buffer = states[slot]
                if step is not None:
                    buffer = buffer + slopes[slot].astype(jnp.float32)
                b_high, b_low = split(buffer)
                dims = ((1,), (0,))
                work[c] = (
                    matmul(turned[0], b_high, dims, None)
                    + matmul(turned[0], b_low, dims, None)
                    + matmul(turned[1], b_high, dims, None)
                )

            copies[0](c).start()

        def stage(offset, action, when=True, low=0, high=chunks):
            c = i - offset

            @pl.when((c >= low) & (c < high) & when)
            def _():
                action(c)

        def paired(c):
            copies[0](c).wait_recv()
            add(work, c, mine, pair, 0, 2 * size)

        def rise_one(c, p):
            @pl.when(away[p] < line - 1)
            def _():
                copies[1 + p](c).wait_recv()

                @pl.when(away[p] > 0)
                def _():
                    add(work, c, one[p], upward.at[p], 0, size)

                @pl.when(away[p] == 0)
                def _():
                    add(fin, c, one[p], upward.at[p], 0, size)

            @pl.when(away[p] > 0)
            def _():
                copies[1 + p](c).start()

        def rise_two(c, p):
            @pl.when(away[p] < line - 1)
            def _():
                copies[3 + p](c).wait_recv()
                add(work, c, two[p], upward.at[p], size, 2 * size)

            @pl.when(away[p] > 0)
            def _():
                copies[3 + p](c).start()

        def exchange(c, p):
            cross[p](c).start()

        def crossed(c, p):
            cross[p](c).wait_recv()
            add(fin, c, two[p], pair, 2 * size, 2 * size)

        def fall(c, p):
            @pl.when(away[p] > 0)
            def _():
                copies[6 + p](c).wait_recv()

            @pl.when(away[p] < line - 1)
            def _():
                copies[6 + p](c).start()

            copies[10 + p](c).start()

            @pl.when(away[p] > 0)
            def _():
                copies[8 + p](c).wait_recv()

            @pl.when(away[p] < line - 1)
            def _():
                copies[8 + p](c).start()

        def gathered(c):
            copies[10](c).wait_recv()
            copies[11](c).wait_recv()

        stage(STRIDE, paired)
        for p in range(2):
            height = (line - 1 - away[p]) * STRIDE
            stage(height, functools.partial(rise_two, p=p))
            stage(STRIDE + height, functools.partial(rise_one, p=p))
        for low, high, later in ((0, first, 0), (first, chunks, delay)):
            for p in range(2):
                at = turn - STRIDE + later // 2
                stage(at, functools.partial(exchange, p=p), away[p] == 0, low, high)
                stage(at + STRIDE, functools.partial(crossed, p=p), away[p] == 0, low, high)
                stage(turn + later + away[p] * STRIDE, functools.partial(fall, p=p), True, low, high)
            stage(2 * turn + later - 1, gathered, True, low, high)

        for t in range(pieces):
            @pl.when(i == begin + t)
            def _():
                if t == 0:
                    gram = jnp.concatenate([fin[k] for k in range(first)], axis=1)
                    factor[...] = 0.5 * (gram + gram.T)
                eliminate(t)

        if ready < total:
            @pl.when(i == ready)
            def _():
                finish()

            @pl.when(i >= ready)
            def _():
                @pl.loop(reached(i - 1), reached(i))
                def _(c):
                    expand(c)

    for t in range(pieces):
        if total <= begin + t:
            if t == 0:
                gram = jnp.concatenate([fin[k] for k in range(first)], axis=1)
                factor[...] = 0.5 * (gram + gram.T)
            eliminate(t)
    if total <= ready:
        finish()

    done = min(max(first + 3 * (total - ready), first), chunks) if ready < total else first

    @pl.loop(done, chunks)
    def _(c):
        expand(c)

    slots[mine_col] = matmul(jnp.ones((8, LANES), jnp.float32), squares[...], ((1,), (1,)), HIGHEST)
    norms = [
        pltpu.make_async_remote_copy(
            src_ref=slots.at[mine_col],
            dst_ref=slots.at[mine_col],
            send_sem=norm_send.at[d],
            recv_sem=norm_recv.at[d],
            device_id={"col": other},
            device_id_type=MESH,
        )
        for d, other in enumerate(others)
    ]
    for copy in norms:
        copy.start()

    @pl.loop(0, chunks)
    def _(c):
        for kind in (0, 10, 11):
            copies[kind](c).wait_send()
        for p in range(2):
            @pl.when(away[p] > 0)
            def _():
                copies[1 + p](c).wait_send()
                copies[3 + p](c).wait_send()

            @pl.when(away[p] == 0)
            def _():
                cross[p](c).wait_send()

            @pl.when(away[p] < line - 1)
            def _():
                copies[6 + p](c).wait_send()
                copies[8 + p](c).wait_send()

    pltpu.make_async_copy(ortho_here, ortho, out_sem.at[chunks - first]).wait()

    @pl.loop(0, chunks - first)
    def _(c):
        pltpu.make_async_copy(raw_here.at[c], raw.at[c], out_sem.at[c]).wait()

    for copy in norms:
        copy.wait()
    whole = slots[0]
    for d in range(1, cols):
        whole = whole + slots[d]
    scale[...] = lax.rsqrt(whole + norm_eps)


def row_reduce(state, grads, step, projected, row_size, col_size, collective_id):
    rows, columns = state.shape
    rank = projected.shape[1]
    chunks = (columns + rank) // WIDTH
    vmem = pl.BlockSpec(memory_space=pltpu.VMEM)
    hbm = pl.BlockSpec(memory_space=pl.ANY)
    size = rank // 8
    f32 = jnp.float32
    operands = (state, projected) if step is None else (state, grads, projected)
    return pl.pallas_call(
        functools.partial(row_kernel, row_size, col_size, step),
        out_shape=[
            jax.ShapeDtypeStruct((rows, rank), f32),
            jax.ShapeDtypeStruct((columns // WIDTH, rank, WIDTH), f32),
            jax.ShapeDtypeStruct((8, rank), f32),
        ],
        in_specs=[hbm] * (len(operands) - 1) + [vmem],
        out_specs=[hbm, hbm, vmem],
        scratch_shapes=[
            pltpu.VMEM((chunks, rank, WIDTH), f32),
            pltpu.VMEM((chunks, rank, WIDTH), f32),
            pltpu.VMEM((2, chunks, 3 * size, WIDTH), f32),
            pltpu.VMEM((chunks, 4 * size, WIDTH), f32),
            pltpu.VMEM((2, rank, rows), jnp.bfloat16),
            pltpu.VMEM((rank, rank), f32),
            pltpu.VMEM((32, LANES), f32),
            pltpu.VMEM((rank, LANES), f32),
            pltpu.VMEM((col_size, 8, rank), f32),
            pltpu.VMEM((SLOTS, rows, WIDTH), f32),
        ]
        + ([] if step is None else [pltpu.VMEM((SLOTS, rows, WIDTH), jnp.bfloat16)])
        + [
            pltpu.VMEM((rows, rank), f32),
            pltpu.VMEM((columns // WIDTH, rank, WIDTH), f32),
            pltpu.SemaphoreType.DMA((2, SLOTS)),
            pltpu.SemaphoreType.DMA((KINDS, chunks)),
            pltpu.SemaphoreType.DMA((KINDS, chunks)),
            pltpu.SemaphoreType.DMA((col_size - 1,)),
            pltpu.SemaphoreType.DMA((col_size - 1,)),
            pltpu.SemaphoreType.DMA((columns // WIDTH + 1,)),
        ],
        compiler_params=pltpu.CompilerParams(
            collective_id=collective_id, has_side_effects=True, vmem_limit_bytes=46 * 2**20
        ),
        cost_estimate=pl.CostEstimate(
            flops=6 * rows * columns * rank, bytes_accessed=6 * rows * columns, transcendentals=0
        ),
    )(*operands)


def project_kernel(cols, step, *refs):
    state, grads, right, refs = *refs[:3], refs[3:]
    if step:
        ortho, scale, refs = *refs[:2], refs[2:]
    projected, refs = refs[0], refs[1:]
    if step:
        buffer, refs = refs[0], refs[1:]
    states, slopes, high, low, part, pair, sums, recvs, refs = *refs[:8], refs[8:]
    if step:
        buffers, left, ortho_here, store_sem, refs = *refs[:4], refs[4:]
    right_here, load_sem, send_sem, recv_sem, right_sem = refs
    tall = states.shape[1]
    rows, rank = projected.shape
    columns = state.shape[1]
    blocks = rows // tall
    half = tall // 2
    bits = cols.bit_length() - 1
    me = lax.axis_index("col")
    partners = [me + (1 - 2 * lax.rem(me // (1 << b), 2)) * (1 << b) for b in range(bits)]
    mine = pl.multiple_of(half * lax.rem(me, 2), 8)
    yours = pl.multiple_of(half * (1 - lax.rem(me, 2)), 8)

    def load(r):
        where = pl.ds(r * tall, tall)
        slot = r % 2
        copies = [pltpu.make_async_copy(state.at[where], states.at[slot], load_sem.at[0, slot])]
        for g in range(step + 1):
            copies.append(
                pltpu.make_async_copy(grads.at[g, where], slopes.at[slot, g], load_sem.at[1 + g, slot])
            )
        return copies

    fetch = [pltpu.make_async_copy(right, right_here, right_sem.at[0])]
    if step:
        fetch.append(pltpu.make_async_copy(ortho, ortho_here, right_sem.at[1]))
    for copy in fetch + load(0):
        copy.start()

    barrier = pltpu.get_barrier_semaphore()
    for partner in partners:
        pl.semaphore_signal(barrier, inc=1, device_id={"col": partner}, device_id_type=MESH)

    for copy in fetch:
        copy.wait()
    if step:
        for c in range(columns // WIDTH):
            at = slice(c * WIDTH, (c + 1) * WIDTH)
            high[:, at], low[:, at] = split(right_here[c])
        left[...] = ortho_here[...].astype(jnp.bfloat16)
    else:
        high[...], low[...] = split(right_here[...])

    pl.semaphore_wait(barrier, bits)

    def remote(kind, r, source, target, partner):
        return pltpu.make_async_remote_copy(
            src_ref=source,
            dst_ref=target,
            send_sem=send_sem.at[kind, r],
            recv_sem=recv_sem.at[kind, r],
            device_id={"col": partner},
            device_id_type=MESH,
        )

    def swap(r):
        return remote(0, r, part.at[r, pl.ds(yours, half)], pair.at[r], partners[0])

    def cross(b, r):
        return remote(b, r, sums.at[b - 1, r], recvs.at[b - 1, r], partners[b])

    def whole(r):
        return projected.at[pl.ds(pl.multiple_of(r * tall + mine, 8), half)]

    def gather(r):
        return remote(bits, r, whole(r), whole(r), partners[0])

    def arrive(k, r):
        if k == 1:
            swap(r).wait_recv()
            value = part[r, pl.ds(mine, half), :] + pair[r]
        else:
            cross(k - 1, r).wait_recv()
            value = sums[k - 2, r] + recvs[k - 2, r]
        if k < bits:
            sums[k - 1, r] = value
            cross(k, r).start()
        else:
            if step:
                value = value * scale[0:1, :]
            whole(r)[...] = value
            gather(r).start()

    deep = min(columns, 2048)
    due = {1 + LAG * (k - 1): k for k in range(1, bits + 1)}
    for t in range(blocks + max(due)):
        if t < blocks:
            slot = t % 2
            if t + 1 < blocks:
                for copy in load(t + 1):
                    copy.start()
            for copy in load(t):
                copy.wait()
            if step and t >= 2:
                store(t - 2).wait()
            part[t] = jnp.zeros(part.shape[1:], jnp.float32)

            @pl.loop(0, columns // deep)
            def _(k):
                at = pl.ds(pl.multiple_of(k * deep, deep), deep)
                value = states[slot, :, at] + slopes[slot, 0, :, at].astype(jnp.float32)
                if step:
                    update = matmul(left[t * tall : (t + 1) * tall, :], high[:, at], ((1,), (0,)), None)
                    value = value - (1.0 - keep_rate) * update
                    value = value + slopes[slot, 1, :, at].astype(jnp.float32)
                    buffers[slot, :, at] = value
                    r_high, r_low, dims = high[:, at], low[:, at], ((1,), (1,))
                else:
                    r_high, r_low, dims = high[at, :], low[at, :], ((1,), (0,))
                v_high, v_low = split(value)
                part[t] += (
                    matmul(v_high, r_high, dims, None)
                    + matmul(v_low, r_high, dims, None)
                    + matmul(v_high, r_low, dims, None)
                )

            if step:
                def store(r):
                    return pltpu.make_async_copy(
                        buffers.at[r % 2], buffer.at[pl.ds(r * tall, tall)], store_sem.at[r % 2]
                    )

                store(t).start()
            swap(t).start()
        for r in range(blocks):
            if t - r in due:
                arrive(due[t - r], r)

    for r in range(blocks):
        swap(r).wait_send()
        gather(r).wait()
        for b in range(1, bits):
            cross(b, r).wait_send()
        if step and r >= blocks - 2:
            store(r).wait()


def project(state, grads, step, right, ortho, scale, col_size, collective_id):
    rows, columns = state.shape
    rank = right.shape[1]
    tall = min(256 if step else 128, rows)
    blocks = rows // tall
    bits = col_size.bit_length() - 1
    vmem = pl.BlockSpec(memory_space=pltpu.VMEM)
    hbm = pl.BlockSpec(memory_space=pl.ANY)
    f32, bf16 = jnp.float32, jnp.bfloat16
    operands = (state, grads, right) + ((ortho, scale) if step else ())
    shape = (rank, columns) if step else (columns, rank)
    out_shape = [jax.ShapeDtypeStruct((rows, rank), f32)]
    scratch = [
        pltpu.VMEM((2, tall, columns), f32),
        pltpu.VMEM((2, step + 1, tall, columns), bf16),
        pltpu.VMEM(shape, bf16),
        pltpu.VMEM(shape, bf16),
        pltpu.VMEM((blocks, tall, rank), f32),
        pltpu.VMEM((blocks, tall // 2, rank), f32),
        pltpu.VMEM((bits - 1, blocks, tall // 2, rank), f32),
        pltpu.VMEM((bits - 1, blocks, tall // 2, rank), f32),
    ]
    if step:
        out_shape.append(jax.ShapeDtypeStruct((rows, columns), f32))
        scratch += [
            pltpu.VMEM((2, tall, columns), f32),
            pltpu.VMEM((rows, rank), bf16),
            pltpu.VMEM((rows, rank), f32),
            pltpu.SemaphoreType.DMA((2,)),
        ]
    return pl.pallas_call(
        functools.partial(project_kernel, col_size, step),
        out_shape=out_shape,
        in_specs=[hbm] * 3 + ([hbm, vmem] if step else []),
        out_specs=[vmem, hbm][: step + 1],
        scratch_shapes=scratch
        + [
            pltpu.VMEM(right.shape, f32),
            pltpu.SemaphoreType.DMA((2 + step, 2)),
            pltpu.SemaphoreType.DMA((bits + 1, blocks)),
            pltpu.SemaphoreType.DMA((bits + 1, blocks)),
            pltpu.SemaphoreType.DMA((1 + step,)),
        ],
        compiler_params=pltpu.CompilerParams(
            collective_id=collective_id, has_side_effects=True, vmem_limit_bytes=52 * 2**20
        ),
        cost_estimate=pl.CostEstimate(
            flops=8 * rows * columns * rank, bytes_accessed=10 * rows * columns, transcendentals=0
        ),
    )(*operands)


def finish_kernel(gain, buffer, ortho, raw, scale, left, right, before, change, state, lefts, highs, news, olds):
    c = pl.program_id(1)
    pieces = raw.shape[0]

    @pl.when((pl.program_id(0) == 0) & (c == 0))
    def _():
        lefts[0, 0], lefts[0, 1] = split(left[...] * (before[0:1, :] * gain))
        lefts[1, 0], lefts[1, 1] = split(ortho[...] * (scale[0:1, :] * gain))
        highs[...] = ortho[...].astype(jnp.bfloat16)

    @pl.when(pl.program_id(0) == 0)
    def _():
        for k in range(pieces):
            news[c * pieces + k, 0], news[c * pieces + k, 1] = split(raw[k])
            olds[c * pieces + k, 0], olds[c * pieces + k, 1] = split(right[k])

    dims = ((1,), (0,))
    tall = buffer.shape[0]
    here = pl.ds(pl.multiple_of(pl.program_id(0) * tall, tall), tall)
    for k in range(pieces):
        at = slice(k * WIDTH, (k + 1) * WIDTH)
        r_high, r_low = news[c * pieces + k, 0], news[c * pieces + k, 1]
        p_high, p_low = olds[c * pieces + k, 0], olds[c * pieces + k, 1]
        state[:, at] = buffer[:, at] - (1.0 - keep_rate) * matmul(highs[here, :], r_high, dims, None)
        total = matmul(lefts[0, 0, here, :], p_high, dims, None)
        total = total + matmul(lefts[0, 1, here, :], p_high, dims, None)
        total = total + matmul(lefts[0, 0, here, :], p_low, dims, None)
        total = total + matmul(lefts[1, 0, here, :], r_high, dims, None)
        total = total + matmul(lefts[1, 1, here, :], r_high, dims, None)
        total = total + matmul(lefts[1, 0, here, :], r_low, dims, None)
        change[:, at] = total.astype(jnp.bfloat16)


TILE_ROWS = 1024
TILE_PIECES = 2


def finish(gain, buffer, ortho, raw, scale, left, right, before):
    rows, columns = buffer.shape
    rank = ortho.shape[1]
    bf16 = jnp.bfloat16
    tall, pieces = min(TILE_ROWS, rows), min(TILE_PIECES, columns // WIDTH)
    tile = pl.BlockSpec((tall, pieces * WIDTH), lambda r, c: (r, c))
    last = columns // WIDTH // pieces - 1
    chunk = pl.BlockSpec((pieces, rank, WIDTH), lambda r, c: (jnp.where(r == 0, c, last), 0, 0))
    whole = pl.BlockSpec((rows, rank), lambda r, c: (0, 0))
    row = pl.BlockSpec((8, rank), lambda r, c: (0, 0))
    return pl.pallas_call(
        functools.partial(finish_kernel, gain),
        grid=(rows // tall, columns // WIDTH // pieces),
        out_shape=[
            jax.ShapeDtypeStruct((rows, columns), bf16),
            jax.ShapeDtypeStruct((rows, columns), jnp.float32),
        ],
        in_specs=[tile, whole, chunk, row, whole, chunk, row],
        out_specs=[tile, tile],
        scratch_shapes=[
            pltpu.VMEM((2, 2, rows, rank), bf16),
            pltpu.VMEM((rows, rank), bf16),
            pltpu.VMEM((columns // WIDTH, 2, rank, WIDTH), bf16),
            pltpu.VMEM((columns // WIDTH, 2, rank, WIDTH), bf16),
        ],
        compiler_params=pltpu.CompilerParams(vmem_limit_bytes=48 * 2**20),
        cost_estimate=pl.CostEstimate(
            flops=14 * rows * columns * rank, bytes_accessed=10 * rows * columns, transcendentals=0
        ),
    )(buffer, ortho, raw, scale, left, right, before)


def shards(row_size, col_size, momentum, grads, basis):
    rank = basis.shape[1]
    gain = (momentum.shape[0] * row_size * momentum.shape[1] * col_size / rank) ** 0.5
    (projected,) = project(momentum, grads, 0, basis, None, None, col_size, 0)
    left, right, before = row_reduce(momentum, grads, 0, projected, row_size, col_size, 1)
    projected, buffer = project(momentum, grads, 1, right, left, before, col_size, 2)
    ortho, raw, scale = row_reduce(buffer, None, None, projected, row_size, col_size, 3)
    return tuple(finish(gain, buffer, ortho, raw, scale, left, right, before))


def solution(mesh):
    return jax.shard_map(
        functools.partial(shards, mesh.shape["row"], mesh.shape["col"]),
        mesh=mesh,
        in_specs=(P("row", "col"), P(None, "row", "col"), P("col", None)),
        out_specs=(P("row", "col"), P("row", "col")),
        check_vma=False,
    )
```

```python
import functools

import jax
import jax.numpy as jnp
from jax import lax
from jax.experimental import pallas as pl
from jax.experimental.pallas import tpu as pltpu
from jax.sharding import PartitionSpec as P

keep_rate = 0.95
norm_eps = 1e-06
HIGH = lax.Precision.HIGH
HIGHEST = lax.Precision.HIGHEST
MESH = pl.DeviceIdType.MESH
LANES = 128
STRIDE = 2
SLOTS = 3
WIDTH = 256
LAG = 3
SHARE = 40
EXTRA = 0


def matmul(a, b, dims, precision):
    return lax.dot_general(a, b, (dims, ((), ())), precision=precision, preferred_element_type=jnp.float32)


def split(x):
    high = x.astype(jnp.bfloat16)
    return high, (x - high.astype(jnp.float32)).astype(jnp.bfloat16)


KINDS = 12


def shares(rank):
    size = rank * SHARE // 256 // 8 * 8
    return size, (rank - 4 * size) // 2


def inverse_norms(slots, cols):
    whole = slots[0]
    for d in range(1, cols):
        whole = whole + slots[d]
    return lax.rsqrt(whole + norm_eps)


def row_kernel(rows, cols, step, *refs):
    state, refs = refs[0], refs[1:]
    if step is not None:
        grads, refs = refs[0], refs[1:]
    projected, ortho, raw, scale, refs = *refs[:4], refs[4:]
    fin, work, upward, pair, turned, factor, panel, squares, slots, states, refs = *refs[:10], refs[10:]
    if step is not None:
        slopes, refs = refs[0], refs[1:]
    ortho_here, raw_here, load_sem, send_sem, recv_sem, norm_send, norm_recv, out_sem = refs
    line = rows // 2
    rank = factor.shape[0]
    first = rank // WIDTH
    chunks = fin.shape[0]
    size, wide = shares(rank)
    me = lax.axis_index("row")
    y = lax.rem(me, 2)
    z = me // 2
    partner = me + 1 - 2 * y
    mine = pl.multiple_of(2 * size * y, 8)
    yours = pl.multiple_of(2 * size * (1 - y), 8)
    away = (z, line - 1 - z)
    nearer = (me - 2, me + 2)
    farther = (me + 2, me - 2)
    one = tuple(pl.multiple_of(mine + size * p, 8) for p in range(2))
    two = tuple(4 * size + wide * p for p in range(2))

    def load(j, slot):
        columns = pl.ds(pl.multiple_of(j * WIDTH, WIDTH), WIDTH)
        copies = [pltpu.make_async_copy(state.at[:, columns], states.at[slot], load_sem.at[0, slot])]
        if step is not None:
            copies.append(pltpu.make_async_copy(grads.at[step, :, columns], slopes.at[slot], load_sem.at[1, slot]))
        return copies

    barrier = pltpu.get_barrier_semaphore()
    pl.semaphore_signal(barrier, inc=1, device_id={"row": partner}, device_id_type=MESH)
    for p in range(2):
        @pl.when(away[p] > 0)
        def _():
            pl.semaphore_signal(barrier, inc=1, device_id={"row": nearer[p]}, device_id_type=MESH)

    mine_col = lax.axis_index("col")
    others = [lax.rem(mine_col + d, cols) for d in range(1, cols)] if step is None else []
    for other in others:
        pl.semaphore_signal(barrier, inc=1, device_id={"col": other}, device_id_type=MESH)
    for j in range(SLOTS - 1):
        for copy in load(j, j):
            copy.start()

    def send(kind, c, source, start, target, at, count, device):
        return pltpu.make_async_remote_copy(
            src_ref=source.at[c, pl.ds(start, count)],
            dst_ref=target.at[c, pl.ds(at, count)],
            send_sem=send_sem.at[kind, c],
            recv_sem=recv_sem.at[kind, c],
            device_id={"row": device},
            device_id_type=MESH,
        )

    copies = {0: lambda c: send(0, c, work, yours, pair, 0, 2 * size, partner)}
    for p in range(2):
        n, f, o, t = nearer[p], farther[p], one[p], two[p]
        up = upward.at[p]
        copies[1 + p] = functools.partial(send, 1 + p, source=work, start=o, target=up, at=0, count=size, device=n)
        copies[3 + p] = functools.partial(
            send, 3 + p, source=work, start=t, target=up, at=size, count=wide, device=n
        )
        copies[6 + p] = functools.partial(send, 6 + p, source=fin, start=o, target=fin, at=o, count=size, device=f)
        copies[8 + p] = functools.partial(send, 8 + p, source=fin, start=t, target=fin, at=t, count=wide, device=f)
        copies[10 + p] = functools.partial(
            send, 10 + p, source=fin, start=o, target=fin, at=o, count=size, device=partner
        )
    cross = [
        functools.partial(
            send, 5, source=work, start=two[p], target=pair, at=2 * size, count=wide, device=partner
        )
        for p in range(2)
    ]

    def add(target, c, start, source, at, count):
        target[c, pl.ds(start, count), :] = work[c, pl.ds(start, count), :] + source[c, pl.ds(at, count), :]

    transposed = projected[...].T
    high, low = split(transposed)
    turned[0] = high
    turned[1] = low
    gram = matmul(transposed, transposed, ((1,), (1,)), HIGHEST)
    for k in range(first):
        work[k] = gram[:, k * WIDTH : (k + 1) * WIDTH]

    pl.semaphore_wait(barrier, jnp.where((z == 0) | (z == line - 1), 2, 3) + len(others))

    turn = line * STRIDE
    delay = max(turn, chunks + 1 - 2 * STRIDE + EXTRA) - turn
    last = 2 * turn + delay

    block = 32
    per = 16
    pieces = rank // per
    begin = 2 * turn + first

    def eliminate(t):
        k0 = (t * per // block) * block
        part = t % (block // per)
        tile = (k0 // LANES) * LANES
        shift = k0 % LANES
        r = lax.broadcasted_iota(jnp.int32, (block, LANES), 0)
        l = lax.broadcasted_iota(jnp.int32, (block, LANES), 1)
        if part == 0:
            d = factor[k0 : k0 + block, tile : tile + LANES]
            if shift:
                d = pltpu.roll(d, LANES - shift, 1)
            aug = jnp.where(l < block, d, jnp.where(l - block == r, 1.0, 0.0))
        else:
            aug = panel[...]
        for j in range(part * per, (part + 1) * per):
            column = jnp.broadcast_to(aug[:, j : j + 1], (block, LANES))
            pivot = column[j : j + 1, :]
            ratio = jnp.where(r > j, column * (1.0 / pivot), 0.0)
            aug = aug - ratio * aug[j : j + 1, :]
        if part < block // per - 1:
            panel[...] = aug
            return
        diagonal = jnp.sum(jnp.where(l == r, aug, 0.0), axis=1, keepdims=True)
        t_inv = (aug * lax.rsqrt(diagonal))[:, block : 2 * block]
        rw = lax.broadcasted_iota(jnp.int32, (block, rank), 0)
        lw = lax.broadcasted_iota(jnp.int32, (block, rank), 1)
        inside = (lw >= k0) & (lw < k0 + block)
        own = jnp.where(inside, jnp.where(lw - k0 == rw, 1.0, 0.0), factor[k0 : k0 + block, :])
        done = matmul(t_inv, own, ((1,), (0,)), HIGHEST)
        factor[k0 : k0 + block, :] = done
        rest = rank - k0 - block
        if rest:
            below = factor[k0 + block :, :]
            left_part = matmul(below[:, k0 : k0 + block], t_inv, ((1,), (1,)), HIGHEST)
            lb = lax.broadcasted_iota(jnp.int32, (rest, rank), 1)
            kept = jnp.where((lb >= k0) & (lb < k0 + block), 0.0, below)
            factor[k0 + block :, :] = kept - matmul(left_part, done, ((1,), (0,)), HIGHEST)

    def finish():
        r = lax.broadcasted_iota(jnp.int32, (rank, rank), 0)
        l = lax.broadcasted_iota(jnp.int32, (rank, rank), 1)
        inverse = jnp.where(l <= r, factor[...], 0.0)
        high, low = split(inverse)
        turned[0, :, :rank] = high
        turned[1, :, :rank] = low
        ortho_here[...] = matmul(projected[...], inverse, ((1,), (1,)), HIGHEST)
        pltpu.make_async_copy(ortho_here, ortho, out_sem.at[chunks - first]).start()
        squares[...] = jnp.zeros_like(squares)

    def expand(c):
        t_high, t_low = split(fin[c])
        i_high, i_low = turned[0, :, :rank], turned[1, :, :rank]
        dims = ((1,), (0,))
        value = matmul(i_high, t_high, dims, None) + matmul(i_high, t_low, dims, None) + matmul(i_low, t_high, dims, None)
        raw_here[c - first] = value
        pltpu.make_async_copy(raw_here.at[c - first], raw.at[c - first], out_sem.at[c - first]).start()
        square = value * value
        squares[...] += sum(square[:, k : k + LANES] for k in range(0, WIDTH, LANES))

    total = chunks + last
    ready = max(begin + pieces, chunks)

    def reached(i):
        count = jnp.minimum(jnp.minimum(first + 3 * (i - ready + 1), i - (last - 1) + 1), chunks)
        return jnp.maximum(count, first)

    @pl.loop(0, total)
    def _(i):
        @pl.when(i < chunks)
        def _():
            c = i

            @pl.when(c >= first)
            def _():
                j = c - first
                slot = lax.rem(j, SLOTS)
                ahead = j + SLOTS - 1

                @pl.when(ahead < chunks - first)
                def _():
                    for copy in load(ahead, lax.rem(ahead, SLOTS)):
                        copy.start()

                for copy in load(j, slot):
                    copy.wait()
                buffer = states[slot]
                if step is not None:
                    buffer = buffer + slopes[slot].astype(jnp.float32)
                b_high, b_low = split(buffer)
                dims = ((1,), (0,))
                work[c] = (
                    matmul(turned[0], b_high, dims, None)
                    + matmul(turned[0], b_low, dims, None)
                    + matmul(turned[1], b_high, dims, None)
                )

            copies[0](c).start()

        def stage(offset, action, when=True, low=0, high=chunks):
            c = i - offset

            @pl.when((c >= low) & (c < high) & when)
            def _():
                action(c)

        def paired(c):
            copies[0](c).wait_recv()
            add(work, c, mine, pair, 0, 2 * size)

        def rise_one(c, p):
            @pl.when(away[p] < line - 1)
            def _():
                copies[1 + p](c).wait_recv()

                @pl.when(away[p] > 0)
                def _():
                    add(work, c, one[p], upward.at[p], 0, size)

                @pl.when(away[p] == 0)
                def _():
                    add(fin, c, one[p], upward.at[p], 0, size)

            @pl.when(away[p] > 0)
            def _():
                copies[1 + p](c).start()

        def rise_two(c, p):
            @pl.when(away[p] < line - 1)
            def _():
                copies[3 + p](c).wait_recv()
                add(work, c, two[p], upward.at[p], size, wide)

            @pl.when(away[p] > 0)
            def _():
                copies[3 + p](c).start()

        def exchange(c, p):
            cross[p](c).start()

        def crossed(c, p):
            cross[p](c).wait_recv()
            add(fin, c, two[p], pair, 2 * size, wide)

        def fall(c, p):
            @pl.when(away[p] > 0)
            def _():
                copies[6 + p](c).wait_recv()

            @pl.when(away[p] < line - 1)
            def _():
                copies[6 + p](c).start()

            copies[10 + p](c).start()

            @pl.when(away[p] > 0)
            def _():
                copies[8 + p](c).wait_recv()

            @pl.when(away[p] < line - 1)
            def _():
                copies[8 + p](c).start()

        def gathered(c):
            copies[10](c).wait_recv()
            copies[11](c).wait_recv()

        stage(STRIDE, paired)
        for p in range(2):
            height = (line - 1 - away[p]) * STRIDE
            stage(height, functools.partial(rise_two, p=p))
            stage(STRIDE + height, functools.partial(rise_one, p=p))
        for low, high, later in ((0, first, 0), (first, chunks, delay)):
            for p in range(2):
                at = turn - STRIDE + later // 2
                stage(at, functools.partial(exchange, p=p), away[p] == 0, low, high)
                stage(at + STRIDE, functools.partial(crossed, p=p), away[p] == 0, low, high)
                stage(turn + later + away[p] * STRIDE, functools.partial(fall, p=p), True, low, high)
            stage(2 * turn + later - 1, gathered, True, low, high)

        for t in range(pieces):
            @pl.when(i == begin + t)
            def _():
                if t == 0:
                    gram = jnp.concatenate([fin[k] for k in range(first)], axis=1)
                    factor[...] = 0.5 * (gram + gram.T)
                eliminate(t)

        if ready < total:
            @pl.when(i == ready)
            def _():
                finish()

            @pl.when(i >= ready)
            def _():
                @pl.loop(reached(i - 1), reached(i))
                def _(c):
                    expand(c)

    for t in range(pieces):
        if total <= begin + t:
            if t == 0:
                gram = jnp.concatenate([fin[k] for k in range(first)], axis=1)
                factor[...] = 0.5 * (gram + gram.T)
            eliminate(t)
    if total <= ready:
        finish()

    done = min(max(first + 3 * (total - ready), first), chunks) if ready < total else first

    @pl.loop(done, chunks)
    def _(c):
        expand(c)

    own = matmul(jnp.ones((8, LANES), jnp.float32), squares[...], ((1,), (1,)), HIGHEST)
    if step is None:
        slots[mine_col] = own
    else:
        scale[...] = own
    norms = [
        pltpu.make_async_remote_copy(
            src_ref=slots.at[mine_col],
            dst_ref=slots.at[mine_col],
            send_sem=norm_send.at[d],
            recv_sem=norm_recv.at[d],
            device_id={"col": other},
            device_id_type=MESH,
        )
        for d, other in enumerate(others)
    ]
    for copy in norms:
        copy.start()

    @pl.loop(0, chunks)
    def _(c):
        for kind in (0, 10, 11):
            copies[kind](c).wait_send()
        for p in range(2):
            @pl.when(away[p] > 0)
            def _():
                copies[1 + p](c).wait_send()
                copies[3 + p](c).wait_send()

            @pl.when(away[p] == 0)
            def _():
                cross[p](c).wait_send()

            @pl.when(away[p] < line - 1)
            def _():
                copies[6 + p](c).wait_send()
                copies[8 + p](c).wait_send()

    pltpu.make_async_copy(ortho_here, ortho, out_sem.at[chunks - first]).wait()

    @pl.loop(0, chunks - first)
    def _(c):
        pltpu.make_async_copy(raw_here.at[c], raw.at[c], out_sem.at[c]).wait()

    if step is None:
        for copy in norms:
            copy.wait()
        scale[...] = inverse_norms(slots, cols)


def row_reduce(state, grads, step, projected, row_size, col_size, collective_id):
    rows, columns = state.shape
    rank = projected.shape[1]
    chunks = (columns + rank) // WIDTH
    vmem = pl.BlockSpec(memory_space=pltpu.VMEM)
    hbm = pl.BlockSpec(memory_space=pltpu.HBM)
    size, wide = shares(rank)
    f32 = jnp.float32
    operands = (state, projected) if step is None else (state, grads, projected)
    return pl.pallas_call(
        functools.partial(row_kernel, row_size, col_size, step),
        out_shape=[
            jax.ShapeDtypeStruct((rows, rank), f32),
            jax.ShapeDtypeStruct((columns // WIDTH, rank, WIDTH), f32),
            jax.ShapeDtypeStruct((8, rank), f32),
        ],
        in_specs=[hbm] * (len(operands) - 1) + [vmem],
        out_specs=[hbm, hbm, vmem],
        scratch_shapes=[
            pltpu.VMEM((chunks, rank, WIDTH), f32),
            pltpu.VMEM((chunks, rank, WIDTH), f32),
            pltpu.VMEM((2, chunks, size + wide, WIDTH), f32),
            pltpu.VMEM((chunks, 2 * size + wide, WIDTH), f32),
            pltpu.VMEM((2, rank, rows), jnp.bfloat16),
            pltpu.VMEM((rank, rank), f32),
            pltpu.VMEM((32, LANES), f32),
            pltpu.VMEM((rank, LANES), f32),
            pltpu.VMEM((col_size, 8, rank), f32),
            pltpu.VMEM((SLOTS, rows, WIDTH), f32),
        ]
        + ([] if step is None else [pltpu.VMEM((SLOTS, rows, WIDTH), jnp.bfloat16)])
        + [
            pltpu.VMEM((rows, rank), f32),
            pltpu.VMEM((columns // WIDTH, rank, WIDTH), f32),
            pltpu.SemaphoreType.DMA((2, SLOTS)),
            pltpu.SemaphoreType.DMA((KINDS, chunks)),
            pltpu.SemaphoreType.DMA((KINDS, chunks)),
            pltpu.SemaphoreType.DMA((col_size - 1,)),
            pltpu.SemaphoreType.DMA((col_size - 1,)),
            pltpu.SemaphoreType.DMA((columns // WIDTH + 1,)),
        ],
        compiler_params=pltpu.CompilerParams(
            collective_id=collective_id, has_side_effects=True, vmem_limit_bytes=62 * 2**20
        ),
        cost_estimate=pl.CostEstimate(
            flops=6 * rows * columns * rank, bytes_accessed=6 * rows * columns, transcendentals=0
        ),
    )(*operands)


def project_kernel(cols, step, *refs):
    state, grads, right, refs = *refs[:3], refs[3:]
    if step:
        ortho, norms, refs = *refs[:2], refs[2:]
    projected, refs = refs[0], refs[1:]
    if step:
        buffer, scale, refs = *refs[:2], refs[2:]
    states, slopes, high, low, part, pair, sums, recvs, refs = *refs[:8], refs[8:]
    if step:
        buffers, left, ortho_here, slots, store_sem, norm_send, norm_recv, refs = *refs[:7], refs[7:]
    right_here, load_sem, send_sem, recv_sem, right_sem = refs
    tall = states.shape[1]
    rows, rank = projected.shape
    columns = state.shape[1]
    blocks = rows // tall
    half = tall // 2
    bits = cols.bit_length() - 1
    me = lax.axis_index("col")
    partners = [me + (1 - 2 * lax.rem(me // (1 << b), 2)) * (1 << b) for b in range(bits)]
    mine = pl.multiple_of(half * lax.rem(me, 2), 8)
    yours = pl.multiple_of(half * (1 - lax.rem(me, 2)), 8)

    def load(r):
        where = pl.ds(r * tall, tall)
        slot = r % 2
        copies = [pltpu.make_async_copy(state.at[where], states.at[slot], load_sem.at[0, slot])]
        for g in range(step + 1):
            copies.append(
                pltpu.make_async_copy(grads.at[g, where], slopes.at[slot, g], load_sem.at[1 + g, slot])
            )
        return copies

    fetch = [pltpu.make_async_copy(right, right_here, right_sem.at[0])]
    if step:
        fetch.append(pltpu.make_async_copy(ortho, ortho_here, right_sem.at[1]))
    for copy in fetch + load(0):
        copy.start()

    barrier = pltpu.get_barrier_semaphore()
    others = [lax.rem(me + d, cols) for d in range(1, cols)] if step else []
    for other in others if step else partners:
        pl.semaphore_signal(barrier, inc=1, device_id={"col": other}, device_id_type=MESH)

    for copy in fetch:
        copy.wait()
    if step:
        for c in range(columns // WIDTH):
            at = slice(c * WIDTH, (c + 1) * WIDTH)
            high[:, at], low[:, at] = split(right_here[c])
        left[...] = ortho_here[...].astype(jnp.bfloat16)
    else:
        high[...], low[...] = split(right_here[...])

    pl.semaphore_wait(barrier, len(others) if step else bits)
    exchange = [
        pltpu.make_async_remote_copy(
            src_ref=norms,
            dst_ref=slots.at[me],
            send_sem=norm_send.at[d],
            recv_sem=norm_recv.at[d],
            device_id={"col": other},
            device_id_type=MESH,
        )
        for d, other in enumerate(others)
    ]
    for copy in exchange:
        copy.start()
    if step:
        slots[me] = norms[...]

    def remote(kind, r, source, target, partner):
        return pltpu.make_async_remote_copy(
            src_ref=source,
            dst_ref=target,
            send_sem=send_sem.at[kind, r],
            recv_sem=recv_sem.at[kind, r],
            device_id={"col": partner},
            device_id_type=MESH,
        )

    def swap(r):
        return remote(0, r, part.at[r, pl.ds(yours, half)], pair.at[r], partners[0])

    def cross(b, r):
        return remote(b, r, sums.at[b - 1, r], recvs.at[b - 1, r], partners[b])

    def whole(r):
        return projected.at[pl.ds(pl.multiple_of(r * tall + mine, 8), half)]

    def gather(r):
        return remote(bits, r, whole(r), whole(r), partners[0])

    def arrive(k, r):
        if k == 1:
            swap(r).wait_recv()
            value = part[r, pl.ds(mine, half), :] + pair[r]
        else:
            cross(k - 1, r).wait_recv()
            value = sums[k - 2, r] + recvs[k - 2, r]
        if k < bits:
            sums[k - 1, r] = value
            cross(k, r).start()
        else:
            if step:
                value = value * scale[0:1, :]
            whole(r)[...] = value
            gather(r).start()

    deep = min(columns, 2048)
    due = {1 + LAG * (k - 1): k for k in range(1, bits + 1)}
    for t in range(blocks + max(due)):
        if t < blocks:
            slot = t % 2
            if t + 1 < blocks:
                for copy in load(t + 1):
                    copy.start()
            for copy in load(t):
                copy.wait()
            if step and t >= 2:
                store(t - 2).wait()
            part[t] = jnp.zeros(part.shape[1:], jnp.float32)

            @pl.loop(0, columns // deep)
            def _(k):
                at = pl.ds(pl.multiple_of(k * deep, deep), deep)
                value = states[slot, :, at] + slopes[slot, 0, :, at].astype(jnp.float32)
                if step:
                    update = matmul(left[t * tall : (t + 1) * tall, :], high[:, at], ((1,), (0,)), None)
                    value = value - (1.0 - keep_rate) * update
                    value = value + slopes[slot, 1, :, at].astype(jnp.float32)
                    buffers[slot, :, at] = value
                    r_high, r_low, dims = high[:, at], low[:, at], ((1,), (1,))
                else:
                    r_high, r_low, dims = high[at, :], low[at, :], ((1,), (0,))
                v_high, v_low = split(value)
                part[t] += (
                    matmul(v_high, r_high, dims, None)
                    + matmul(v_low, r_high, dims, None)
                    + matmul(v_high, r_low, dims, None)
                )

            if step:
                def store(r):
                    return pltpu.make_async_copy(
                        buffers.at[r % 2], buffer.at[pl.ds(r * tall, tall)], store_sem.at[r % 2]
                    )

                store(t).start()
            swap(t).start()
            if step and t == 0:
                for copy in exchange:
                    copy.wait()
                scale[...] = inverse_norms(slots, cols)
        for r in range(blocks):
            if t - r in due:
                arrive(due[t - r], r)

    for r in range(blocks):
        swap(r).wait_send()
        gather(r).wait()
        for b in range(1, bits):
            cross(b, r).wait_send()
        if step and r >= blocks - 2:
            store(r).wait()


def project(state, grads, step, right, ortho, norms, col_size, collective_id):
    rows, columns = state.shape
    rank = right.shape[1]
    tall = min(256 if step else 128, rows)
    blocks = rows // tall
    bits = col_size.bit_length() - 1
    vmem = pl.BlockSpec(memory_space=pltpu.VMEM)
    hbm = pl.BlockSpec(memory_space=pltpu.HBM)
    f32, bf16 = jnp.float32, jnp.bfloat16
    operands = (state, grads, right) + ((ortho, norms) if step else ())
    shape = (rank, columns) if step else (columns, rank)
    out_shape = [jax.ShapeDtypeStruct((rows, rank), f32)]
    scratch = [
        pltpu.VMEM((2, tall, columns), f32),
        pltpu.VMEM((2, step + 1, tall, columns), bf16),
        pltpu.VMEM(shape, bf16),
        pltpu.VMEM(shape, bf16),
        pltpu.VMEM((blocks, tall, rank), f32),
        pltpu.VMEM((blocks, tall // 2, rank), f32),
        pltpu.VMEM((bits - 1, blocks, tall // 2, rank), f32),
        pltpu.VMEM((bits - 1, blocks, tall // 2, rank), f32),
    ]
    if step:
        out_shape += [jax.ShapeDtypeStruct((rows, columns), f32), jax.ShapeDtypeStruct((8, rank), f32)]
        scratch += [
            pltpu.VMEM((2, tall, columns), f32),
            pltpu.VMEM((rows, rank), bf16),
            pltpu.VMEM((rows, rank), f32),
            pltpu.VMEM((col_size, 8, rank), f32),
            pltpu.SemaphoreType.DMA((2,)),
            pltpu.SemaphoreType.DMA((col_size - 1,)),
            pltpu.SemaphoreType.DMA((col_size - 1,)),
        ]
    return pl.pallas_call(
        functools.partial(project_kernel, col_size, step),
        out_shape=out_shape,
        in_specs=[hbm] * 3 + ([hbm, vmem] if step else []),
        out_specs=[vmem, hbm, vmem] if step else [vmem],
        scratch_shapes=scratch
        + [
            pltpu.VMEM(right.shape, f32),
            pltpu.SemaphoreType.DMA((2 + step, 2)),
            pltpu.SemaphoreType.DMA((bits + 1, blocks)),
            pltpu.SemaphoreType.DMA((bits + 1, blocks)),
            pltpu.SemaphoreType.DMA((1 + step,)),
        ],
        compiler_params=pltpu.CompilerParams(
            collective_id=collective_id, has_side_effects=True, vmem_limit_bytes=62 * 2**20
        ),
        cost_estimate=pl.CostEstimate(
            flops=8 * rows * columns * rank, bytes_accessed=10 * rows * columns, transcendentals=0
        ),
    )(*operands)


def finish_kernel(gain, buffer, ortho, raw, scale, left, right, before, change, state, lefts, highs, news, olds):
    c = pl.program_id(1)
    pieces = raw.shape[0]

    @pl.when((pl.program_id(0) == 0) & (c == 0))
    def _():
        lefts[0, 0], lefts[0, 1] = split(left[...] * (before[0:1, :] * gain))
        lefts[1, 0], lefts[1, 1] = split(ortho[...] * (scale[0:1, :] * gain))
        highs[...] = ortho[...].astype(jnp.bfloat16)

    @pl.when(pl.program_id(0) == 0)
    def _():
        for k in range(pieces):
            news[c * pieces + k, 0], news[c * pieces + k, 1] = split(raw[k])
            olds[c * pieces + k, 0], olds[c * pieces + k, 1] = split(right[k])

    dims = ((1,), (0,))
    tall = buffer.shape[0]
    here = pl.ds(pl.multiple_of(pl.program_id(0) * tall, tall), tall)
    for k in range(pieces):
        at = slice(k * WIDTH, (k + 1) * WIDTH)
        r_high, r_low = news[c * pieces + k, 0], news[c * pieces + k, 1]
        p_high, p_low = olds[c * pieces + k, 0], olds[c * pieces + k, 1]
        state[:, at] = buffer[:, at] - (1.0 - keep_rate) * matmul(highs[here, :], r_high, dims, None)
        total = matmul(lefts[0, 0, here, :], p_high, dims, None)
        total = total + matmul(lefts[0, 1, here, :], p_high, dims, None)
        total = total + matmul(lefts[0, 0, here, :], p_low, dims, None)
        total = total + matmul(lefts[1, 0, here, :], r_high, dims, None)
        total = total + matmul(lefts[1, 1, here, :], r_high, dims, None)
        total = total + matmul(lefts[1, 0, here, :], r_low, dims, None)
        change[:, at] = total.astype(jnp.bfloat16)


TILE_ROWS = 1024
TILE_PIECES = 2


def finish(gain, buffer, ortho, raw, scale, left, right, before):
    rows, columns = buffer.shape
    rank = ortho.shape[1]
    bf16 = jnp.bfloat16
    tall, pieces = min(TILE_ROWS, rows), min(TILE_PIECES, columns // WIDTH)
    tile = pl.BlockSpec((tall, pieces * WIDTH), lambda r, c: (r, c))
    last = columns // WIDTH // pieces - 1
    chunk = pl.BlockSpec((pieces, rank, WIDTH), lambda r, c: (jnp.where(r == 0, c, last), 0, 0))
    whole = pl.BlockSpec((rows, rank), lambda r, c: (0, 0))
    row = pl.BlockSpec((8, rank), lambda r, c: (0, 0))
    return pl.pallas_call(
        functools.partial(finish_kernel, gain),
        grid=(rows // tall, columns // WIDTH // pieces),
        out_shape=[
            jax.ShapeDtypeStruct((rows, columns), bf16),
            jax.ShapeDtypeStruct((rows, columns), jnp.float32),
        ],
        in_specs=[tile, whole, chunk, row, whole, chunk, row],
        out_specs=[tile, tile],
        scratch_shapes=[
            pltpu.VMEM((2, 2, rows, rank), bf16),
            pltpu.VMEM((rows, rank), bf16),
            pltpu.VMEM((columns // WIDTH, 2, rank, WIDTH), bf16),
            pltpu.VMEM((columns // WIDTH, 2, rank, WIDTH), bf16),
        ],
        compiler_params=pltpu.CompilerParams(vmem_limit_bytes=48 * 2**20),
        cost_estimate=pl.CostEstimate(
            flops=14 * rows * columns * rank, bytes_accessed=10 * rows * columns, transcendentals=0
        ),
    )(buffer, ortho, raw, scale, left, right, before)


def shards(row_size, col_size, momentum, grads, basis):
    rank = basis.shape[1]
    gain = (momentum.shape[0] * row_size * momentum.shape[1] * col_size / rank) ** 0.5
    (projected,) = project(momentum, grads, 0, basis, None, None, col_size, 0)
    left, right, norms = row_reduce(momentum, grads, 0, projected, row_size, col_size, 1)
    projected, buffer, before = project(momentum, grads, 1, right, left, norms, col_size, 2)
    ortho, raw, scale = row_reduce(buffer, None, None, projected, row_size, col_size, 3)
    return tuple(finish(gain, buffer, ortho, raw, scale, left, right, before))


def solution(mesh):
    return jax.shard_map(
        functools.partial(shards, mesh.shape["row"], mesh.shape["col"]),
        mesh=mesh,
        in_specs=(P("row", "col"), P(None, "row", "col"), P("col", None)),
        out_specs=(P("row", "col"), P("row", "col")),
        check_vma=False,
    )
```

```python
import functools

import jax
import jax.numpy as jnp
from jax import lax
from jax.experimental import pallas as pl
from jax.experimental.pallas import tpu as pltpu
from jax.sharding import PartitionSpec as P

keep_rate = 0.95
norm_eps = 1e-06
HIGH = lax.Precision.HIGH
HIGHEST = lax.Precision.HIGHEST
MESH = pl.DeviceIdType.MESH
LANES = 128
STRIDE = 2
SLOTS = 3
WIDTH = 256
LAG = 3
SHARE = 40
EXTRA = 1


def matmul(a, b, dims, precision):
    return lax.dot_general(a, b, (dims, ((), ())), precision=precision, preferred_element_type=jnp.float32)


def split(x):
    high = x.astype(jnp.bfloat16)
    return high, (x - high.astype(jnp.float32)).astype(jnp.bfloat16)


KINDS = 12


def shares(rank):
    size = rank * SHARE // 256 // 8 * 8
    return size, (rank - 4 * size) // 2


def inverse_norms(slots, cols):
    whole = slots[0]
    for d in range(1, cols):
        whole = whole + slots[d]
    return lax.rsqrt(whole + norm_eps)


def row_kernel(rows, cols, step, *refs):
    state, refs = refs[0], refs[1:]
    if step is not None:
        grads, refs = refs[0], refs[1:]
    projected, ortho, raw, scale, refs = *refs[:4], refs[4:]
    fin, work, upward, pair, turned, factor, panel, squares, slots, states, refs = *refs[:10], refs[10:]
    if step is not None:
        slopes, refs = refs[0], refs[1:]
    ortho_here, raw_here, load_sem, send_sem, recv_sem, norm_send, norm_recv, out_sem = refs
    line = rows // 2
    rank = factor.shape[0]
    first = rank // WIDTH
    chunks = fin.shape[0]
    size, wide = shares(rank)
    me = lax.axis_index("row")
    y = lax.rem(me, 2)
    z = me // 2
    partner = me + 1 - 2 * y
    mine = pl.multiple_of(2 * size * y, 8)
    yours = pl.multiple_of(2 * size * (1 - y), 8)
    away = (z, line - 1 - z)
    nearer = (me - 2, me + 2)
    farther = (me + 2, me - 2)
    one = tuple(pl.multiple_of(mine + size * p, 8) for p in range(2))
    two = tuple(4 * size + wide * p for p in range(2))

    def load(j, slot):
        columns = pl.ds(pl.multiple_of(j * WIDTH, WIDTH), WIDTH)
        copies = [pltpu.make_async_copy(state.at[:, columns], states.at[slot], load_sem.at[0, slot])]
        if step is not None:
            copies.append(pltpu.make_async_copy(grads.at[step, :, columns], slopes.at[slot], load_sem.at[1, slot]))
        return copies

    barrier = pltpu.get_barrier_semaphore()
    pl.semaphore_signal(barrier, inc=1, device_id={"row": partner}, device_id_type=MESH)
    for p in range(2):
        @pl.when(away[p] > 0)
        def _():
            pl.semaphore_signal(barrier, inc=1, device_id={"row": nearer[p]}, device_id_type=MESH)

    mine_col = lax.axis_index("col")
    others = [lax.rem(mine_col + d, cols) for d in range(1, cols)] if step is None else []
    for other in others:
        pl.semaphore_signal(barrier, inc=1, device_id={"col": other}, device_id_type=MESH)
    for j in range(SLOTS - 1):
        for copy in load(j, j):
            copy.start()

    def send(kind, c, source, start, target, at, count, device):
        return pltpu.make_async_remote_copy(
            src_ref=source.at[c, pl.ds(start, count)],
            dst_ref=target.at[c, pl.ds(at, count)],
            send_sem=send_sem.at[kind, c],
            recv_sem=recv_sem.at[kind, c],
            device_id={"row": device},
            device_id_type=MESH,
        )

    copies = {0: lambda c: send(0, c, work, yours, pair, 0, 2 * size, partner)}
    for p in range(2):
        n, f, o, t = nearer[p], farther[p], one[p], two[p]
        up = upward.at[p]
        copies[1 + p] = functools.partial(send, 1 + p, source=work, start=o, target=up, at=0, count=size, device=n)
        copies[3 + p] = functools.partial(
            send, 3 + p, source=work, start=t, target=up, at=size, count=wide, device=n
        )
        copies[6 + p] = functools.partial(send, 6 + p, source=fin, start=o, target=fin, at=o, count=size, device=f)
        copies[8 + p] = functools.partial(send, 8 + p, source=fin, start=t, target=fin, at=t, count=wide, device=f)
        copies[10 + p] = functools.partial(
            send, 10 + p, source=fin, start=o, target=fin, at=o, count=size, device=partner
        )
    cross = [
        functools.partial(
            send, 5, source=work, start=two[p], target=pair, at=2 * size, count=wide, device=partner
        )
        for p in range(2)
    ]

    def add(target, c, start, source, at, count):
        target[c, pl.ds(start, count), :] = work[c, pl.ds(start, count), :] + source[c, pl.ds(at, count), :]

    transposed = projected[...].T
    high, low = split(transposed)
    turned[0] = high
    turned[1] = low
    gram = matmul(transposed, transposed, ((1,), (1,)), HIGHEST)
    for k in range(first):
        work[k] = gram[:, k * WIDTH : (k + 1) * WIDTH]

    pl.semaphore_wait(barrier, jnp.where((z == 0) | (z == line - 1), 2, 3) + len(others))

    turn = line * STRIDE
    delay = max(turn, chunks + 1 - 2 * STRIDE + EXTRA) - turn
    last = 2 * turn + delay

    block = 32
    per = 16
    pieces = rank // per
    begin = 2 * turn + first

    def eliminate(t):
        k0 = (t * per // block) * block
        part = t % (block // per)
        tile = (k0 // LANES) * LANES
        shift = k0 % LANES
        r = lax.broadcasted_iota(jnp.int32, (block, LANES), 0)
        l = lax.broadcasted_iota(jnp.int32, (block, LANES), 1)
        if part == 0:
            d = factor[k0 : k0 + block, tile : tile + LANES]
            if shift:
                d = pltpu.roll(d, LANES - shift, 1)
            aug = jnp.where(l < block, d, jnp.where(l - block == r, 1.0, 0.0))
        else:
            aug = panel[...]
        for j in range(part * per, (part + 1) * per):
            column = jnp.broadcast_to(aug[:, j : j + 1], (block, LANES))
            pivot = column[j : j + 1, :]
            ratio = jnp.where(r > j, column * (1.0 / pivot), 0.0)
            aug = aug - ratio * aug[j : j + 1, :]
        if part < block // per - 1:
            panel[...] = aug
            return
        diagonal = jnp.sum(jnp.where(l == r, aug, 0.0), axis=1, keepdims=True)
        t_inv = (aug * lax.rsqrt(diagonal))[:, block : 2 * block]
        rw = lax.broadcasted_iota(jnp.int32, (block, rank), 0)
        lw = lax.broadcasted_iota(jnp.int32, (block, rank), 1)
        inside = (lw >= k0) & (lw < k0 + block)
        own = jnp.where(inside, jnp.where(lw - k0 == rw, 1.0, 0.0), factor[k0 : k0 + block, :])
        done = matmul(t_inv, own, ((1,), (0,)), HIGHEST)
        factor[k0 : k0 + block, :] = done
        rest = rank - k0 - block
        if rest:
            below = factor[k0 + block :, :]
            left_part = matmul(below[:, k0 : k0 + block], t_inv, ((1,), (1,)), HIGHEST)
            lb = lax.broadcasted_iota(jnp.int32, (rest, rank), 1)
            kept = jnp.where((lb >= k0) & (lb < k0 + block), 0.0, below)
            factor[k0 + block :, :] = kept - matmul(left_part, done, ((1,), (0,)), HIGHEST)

    def finish():
        r = lax.broadcasted_iota(jnp.int32, (rank, rank), 0)
        l = lax.broadcasted_iota(jnp.int32, (rank, rank), 1)
        inverse = jnp.where(l <= r, factor[...], 0.0)
        high, low = split(inverse)
        turned[0, :, :rank] = high
        turned[1, :, :rank] = low
        ortho_here[...] = matmul(projected[...], inverse, ((1,), (1,)), HIGHEST)
        pltpu.make_async_copy(ortho_here, ortho, out_sem.at[chunks - first]).start()
        squares[...] = jnp.zeros_like(squares)

    def expand(c):
        t_high, t_low = split(fin[c])
        i_high, i_low = turned[0, :, :rank], turned[1, :, :rank]
        dims = ((1,), (0,))
        value = matmul(i_high, t_high, dims, None) + matmul(i_high, t_low, dims, None) + matmul(i_low, t_high, dims, None)
        raw_here[c - first] = value
        pltpu.make_async_copy(raw_here.at[c - first], raw.at[c - first], out_sem.at[c - first]).start()
        square = value * value
        squares[...] += sum(square[:, k : k + LANES] for k in range(0, WIDTH, LANES))

    total = chunks + last
    ready = max(begin + pieces, chunks)

    def reached(i):
        count = jnp.minimum(jnp.minimum(first + 3 * (i - ready + 1), i - (last - 1) + 1), chunks)
        return jnp.maximum(count, first)

    @pl.loop(0, total)
    def _(i):
        @pl.when(i < chunks)
        def _():
            c = i

            @pl.when(c >= first)
            def _():
                j = c - first
                slot = lax.rem(j, SLOTS)
                ahead = j + SLOTS - 1

                @pl.when(ahead < chunks - first)
                def _():
                    for copy in load(ahead, lax.rem(ahead, SLOTS)):
                        copy.start()

                for copy in load(j, slot):
                    copy.wait()
                buffer = states[slot]
                if step is not None:
                    buffer = buffer + slopes[slot].astype(jnp.float32)
                b_high, b_low = split(buffer)
                dims = ((1,), (0,))
                work[c] = (
                    matmul(turned[0], b_high, dims, None)
                    + matmul(turned[0], b_low, dims, None)
                    + matmul(turned[1], b_high, dims, None)
                )

            copies[0](c).start()

        def stage(offset, action, when=True, low=0, high=chunks):
            c = i - offset

            @pl.when((c >= low) & (c < high) & when)
            def _():
                action(c)

        def paired(c):
            copies[0](c).wait_recv()
            add(work, c, mine, pair, 0, 2 * size)

        def rise_one(c, p):
            @pl.when(away[p] < line - 1)
            def _():
                copies[1 + p](c).wait_recv()

                @pl.when(away[p] > 0)
                def _():
                    add(work, c, one[p], upward.at[p], 0, size)

                @pl.when(away[p] == 0)
                def _():
                    add(fin, c, one[p], upward.at[p], 0, size)

            @pl.when(away[p] > 0)
            def _():
                copies[1 + p](c).start()

        def rise_two(c, p):
            @pl.when(away[p] < line - 1)
            def _():
                copies[3 + p](c).wait_recv()
                add(work, c, two[p], upward.at[p], size, wide)

            @pl.when(away[p] > 0)
            def _():
                copies[3 + p](c).start()

        def exchange(c, p):
            cross[p](c).start()

        def crossed(c, p):
            cross[p](c).wait_recv()
            add(fin, c, two[p], pair, 2 * size, wide)

        def fall(c, p):
            @pl.when(away[p] > 0)
            def _():
                copies[6 + p](c).wait_recv()

            @pl.when(away[p] < line - 1)
            def _():
                copies[6 + p](c).start()

            copies[10 + p](c).start()

            @pl.when(away[p] > 0)
            def _():
                copies[8 + p](c).wait_recv()

            @pl.when(away[p] < line - 1)
            def _():
                copies[8 + p](c).start()

        def gathered(c):
            copies[10](c).wait_recv()
            copies[11](c).wait_recv()

        stage(STRIDE, paired)
        for p in range(2):
            height = (line - 1 - away[p]) * STRIDE
            stage(height, functools.partial(rise_two, p=p))
            stage(STRIDE + height, functools.partial(rise_one, p=p))
        for low, high, later in ((0, first, 0), (first, chunks, delay)):
            for p in range(2):
                at = turn - STRIDE + later // 2
                stage(at, functools.partial(exchange, p=p), away[p] == 0, low, high)
                stage(at + STRIDE, functools.partial(crossed, p=p), away[p] == 0, low, high)
                stage(turn + later + away[p] * STRIDE, functools.partial(fall, p=p), True, low, high)
            stage(2 * turn + later - 1, gathered, True, low, high)

        for t in range(pieces):
            @pl.when(i == begin + t)
            def _():
                if t == 0:
                    gram = jnp.concatenate([fin[k] for k in range(first)], axis=1)
                    factor[...] = 0.5 * (gram + gram.T)
                eliminate(t)

        if ready < total:
            @pl.when(i == ready)
            def _():
                finish()

            @pl.when(i >= ready)
            def _():
                @pl.loop(reached(i - 1), reached(i))
                def _(c):
                    expand(c)

    for t in range(pieces):
        if total <= begin + t:
            if t == 0:
                gram = jnp.concatenate([fin[k] for k in range(first)], axis=1)
                factor[...] = 0.5 * (gram + gram.T)
            eliminate(t)
    if total <= ready:
        finish()

    done = min(max(first + 3 * (total - ready), first), chunks) if ready < total else first

    @pl.loop(done, chunks)
    def _(c):
        expand(c)

    own = matmul(jnp.ones((8, LANES), jnp.float32), squares[...], ((1,), (1,)), HIGHEST)
    if step is None:
        slots[mine_col] = own
    else:
        scale[...] = own
    norms = [
        pltpu.make_async_remote_copy(
            src_ref=slots.at[mine_col],
            dst_ref=slots.at[mine_col],
            send_sem=norm_send.at[d],
            recv_sem=norm_recv.at[d],
            device_id={"col": other},
            device_id_type=MESH,
        )
        for d, other in enumerate(others)
    ]
    for copy in norms:
        copy.start()

    @pl.loop(0, chunks)
    def _(c):
        for kind in (0, 10, 11):
            copies[kind](c).wait_send()
        for p in range(2):
            @pl.when(away[p] > 0)
            def _():
                copies[1 + p](c).wait_send()
                copies[3 + p](c).wait_send()

            @pl.when(away[p] == 0)
            def _():
                cross[p](c).wait_send()

            @pl.when(away[p] < line - 1)
            def _():
                copies[6 + p](c).wait_send()
                copies[8 + p](c).wait_send()

    pltpu.make_async_copy(ortho_here, ortho, out_sem.at[chunks - first]).wait()

    @pl.loop(0, chunks - first)
    def _(c):
        pltpu.make_async_copy(raw_here.at[c], raw.at[c], out_sem.at[c]).wait()

    if step is None:
        for copy in norms:
            copy.wait()
        scale[...] = inverse_norms(slots, cols)


def row_reduce(state, grads, step, projected, row_size, col_size, collective_id):
    rows, columns = state.shape
    rank = projected.shape[1]
    chunks = (columns + rank) // WIDTH
    vmem = pl.BlockSpec(memory_space=pltpu.VMEM)
    hbm = pl.BlockSpec(memory_space=pltpu.HBM)
    size, wide = shares(rank)
    f32 = jnp.float32
    operands = (state, projected) if step is None else (state, grads, projected)
    return pl.pallas_call(
        functools.partial(row_kernel, row_size, col_size, step),
        out_shape=[
            jax.ShapeDtypeStruct((rows, rank), f32),
            jax.ShapeDtypeStruct((columns // WIDTH, rank, WIDTH), f32),
            jax.ShapeDtypeStruct((8, rank), f32),
        ],
        in_specs=[hbm] * (len(operands) - 1) + [vmem],
        out_specs=[hbm, hbm, vmem],
        scratch_shapes=[
            pltpu.VMEM((chunks, rank, WIDTH), f32),
            pltpu.VMEM((chunks, rank, WIDTH), f32),
            pltpu.VMEM((2, chunks, size + wide, WIDTH), f32),
            pltpu.VMEM((chunks, 2 * size + wide, WIDTH), f32),
            pltpu.VMEM((2, rank, rows), jnp.bfloat16),
            pltpu.VMEM((rank, rank), f32),
            pltpu.VMEM((32, LANES), f32),
            pltpu.VMEM((rank, LANES), f32),
            pltpu.VMEM((col_size, 8, rank), f32),
            pltpu.VMEM((SLOTS, rows, WIDTH), f32),
        ]
        + ([] if step is None else [pltpu.VMEM((SLOTS, rows, WIDTH), jnp.bfloat16)])
        + [
            pltpu.VMEM((rows, rank), f32),
            pltpu.VMEM((columns // WIDTH, rank, WIDTH), f32),
            pltpu.SemaphoreType.DMA((2, SLOTS)),
            pltpu.SemaphoreType.DMA((KINDS, chunks)),
            pltpu.SemaphoreType.DMA((KINDS, chunks)),
            pltpu.SemaphoreType.DMA((col_size - 1,)),
            pltpu.SemaphoreType.DMA((col_size - 1,)),
            pltpu.SemaphoreType.DMA((columns // WIDTH + 1,)),
        ],
        compiler_params=pltpu.CompilerParams(
            collective_id=collective_id, has_side_effects=True, vmem_limit_bytes=62 * 2**20
        ),
        cost_estimate=pl.CostEstimate(
            flops=6 * rows * columns * rank, bytes_accessed=6 * rows * columns, transcendentals=0
        ),
    )(*operands)


def project_kernel(cols, step, *refs):
    state, grads, right, refs = *refs[:3], refs[3:]
    if step:
        ortho, norms, refs = *refs[:2], refs[2:]
    projected, refs = refs[0], refs[1:]
    if step:
        buffer, scale, refs = *refs[:2], refs[2:]
    states, slopes, high, low, part, pair, sums, recvs, refs = *refs[:8], refs[8:]
    if step:
        buffers, left, ortho_here, slots, store_sem, norm_send, norm_recv, refs = *refs[:7], refs[7:]
    right_here, load_sem, send_sem, recv_sem, right_sem = refs
    tall = states.shape[1]
    rows, rank = projected.shape
    columns = state.shape[1]
    blocks = rows // tall
    half = tall // 2
    bits = cols.bit_length() - 1
    me = lax.axis_index("col")
    partners = [me + (1 - 2 * lax.rem(me // (1 << b), 2)) * (1 << b) for b in range(bits)]
    mine = pl.multiple_of(half * lax.rem(me, 2), 8)
    yours = pl.multiple_of(half * (1 - lax.rem(me, 2)), 8)

    def load(r):
        where = pl.ds(r * tall, tall)
        slot = r % 2
        copies = [pltpu.make_async_copy(state.at[where], states.at[slot], load_sem.at[0, slot])]
        for g in range(step + 1):
            copies.append(
                pltpu.make_async_copy(grads.at[g, where], slopes.at[slot, g], load_sem.at[1 + g, slot])
            )
        return copies

    fetch = [pltpu.make_async_copy(right, right_here, right_sem.at[0])]
    if step:
        fetch.append(pltpu.make_async_copy(ortho, ortho_here, right_sem.at[1]))
    for copy in fetch + load(0):
        copy.start()

    barrier = pltpu.get_barrier_semaphore()
    others = [lax.rem(me + d, cols) for d in range(1, cols)] if step else []
    for other in others if step else partners:
        pl.semaphore_signal(barrier, inc=1, device_id={"col": other}, device_id_type=MESH)

    for copy in fetch:
        copy.wait()
    if step:
        for c in range(columns // WIDTH):
            at = slice(c * WIDTH, (c + 1) * WIDTH)
            high[:, at], low[:, at] = split(right_here[c])
        left[...] = ortho_here[...].astype(jnp.bfloat16)
    else:
        high[...], low[...] = split(right_here[...])

    pl.semaphore_wait(barrier, len(others) if step else bits)
    exchange = [
        pltpu.make_async_remote_copy(
            src_ref=norms,
            dst_ref=slots.at[me],
            send_sem=norm_send.at[d],
            recv_sem=norm_recv.at[d],
            device_id={"col": other},
            device_id_type=MESH,
        )
        for d, other in enumerate(others)
    ]
    for copy in exchange:
        copy.start()
    if step:
        slots[me] = norms[...]

    def remote(kind, r, source, target, partner):
        return pltpu.make_async_remote_copy(
            src_ref=source,
            dst_ref=target,
            send_sem=send_sem.at[kind, r],
            recv_sem=recv_sem.at[kind, r],
            device_id={"col": partner},
            device_id_type=MESH,
        )

    def swap(r):
        return remote(0, r, part.at[r, pl.ds(yours, half)], pair.at[r], partners[0])

    def cross(b, r):
        return remote(b, r, sums.at[b - 1, r], recvs.at[b - 1, r], partners[b])

    def whole(r):
        return projected.at[pl.ds(pl.multiple_of(r * tall + mine, 8), half)]

    def gather(r):
        return remote(bits, r, whole(r), whole(r), partners[0])

    def arrive(k, r):
        if k == 1:
            swap(r).wait_recv()
            value = part[r, pl.ds(mine, half), :] + pair[r]
        else:
            cross(k - 1, r).wait_recv()
            value = sums[k - 2, r] + recvs[k - 2, r]
        if k < bits:
            sums[k - 1, r] = value
            cross(k, r).start()
        else:
            if step:
                value = value * scale[0:1, :]
            whole(r)[...] = value
            gather(r).start()

    deep = min(columns, 2048)
    due = {1 + LAG * (k - 1): k for k in range(1, bits + 1)}
    for t in range(blocks + max(due)):
        if t < blocks:
            slot = t % 2
            if t + 1 < blocks:
                for copy in load(t + 1):
                    copy.start()
            for copy in load(t):
                copy.wait()
            if step and t >= 2:
                store(t - 2).wait()
            part[t] = jnp.zeros(part.shape[1:], jnp.float32)

            @pl.loop(0, columns // deep)
            def _(k):
                at = pl.ds(pl.multiple_of(k * deep, deep), deep)
                value = states[slot, :, at] + slopes[slot, 0, :, at].astype(jnp.float32)
                if step:
                    update = matmul(left[t * tall : (t + 1) * tall, :], high[:, at], ((1,), (0,)), None)
                    value = value - (1.0 - keep_rate) * update
                    value = value + slopes[slot, 1, :, at].astype(jnp.float32)
                    buffers[slot, :, at] = value
                    r_high, r_low, dims = high[:, at], low[:, at], ((1,), (1,))
                else:
                    r_high, r_low, dims = high[at, :], low[at, :], ((1,), (0,))
                v_high, v_low = split(value)
                part[t] += (
                    matmul(v_high, r_high, dims, None)
                    + matmul(v_low, r_high, dims, None)
                    + matmul(v_high, r_low, dims, None)
                )

            if step:
                def store(r):
                    return pltpu.make_async_copy(
                        buffers.at[r % 2], buffer.at[pl.ds(r * tall, tall)], store_sem.at[r % 2]
                    )

                store(t).start()
            swap(t).start()
            if step and t == 0:
                for copy in exchange:
                    copy.wait()
                scale[...] = inverse_norms(slots, cols)
        for r in range(blocks):
            if t - r in due:
                arrive(due[t - r], r)

    for r in range(blocks):
        swap(r).wait_send()
        gather(r).wait()
        for b in range(1, bits):
            cross(b, r).wait_send()
        if step and r >= blocks - 2:
            store(r).wait()


def project(state, grads, step, right, ortho, norms, col_size, collective_id):
    rows, columns = state.shape
    rank = right.shape[1]
    tall = min(256 if step else 128, rows)
    blocks = rows // tall
    bits = col_size.bit_length() - 1
    vmem = pl.BlockSpec(memory_space=pltpu.VMEM)
    hbm = pl.BlockSpec(memory_space=pltpu.HBM)
    f32, bf16 = jnp.float32, jnp.bfloat16
    operands = (state, grads, right) + ((ortho, norms) if step else ())
    shape = (rank, columns) if step else (columns, rank)
    out_shape = [jax.ShapeDtypeStruct((rows, rank), f32)]
    scratch = [
        pltpu.VMEM((2, tall, columns), f32),
        pltpu.VMEM((2, step + 1, tall, columns), bf16),
        pltpu.VMEM(shape, bf16),
        pltpu.VMEM(shape, bf16),
        pltpu.VMEM((blocks, tall, rank), f32),
        pltpu.VMEM((blocks, tall // 2, rank), f32),
        pltpu.VMEM((bits - 1, blocks, tall // 2, rank), f32),
        pltpu.VMEM((bits - 1, blocks, tall // 2, rank), f32),
    ]
    if step:
        out_shape += [jax.ShapeDtypeStruct((rows, columns), f32), jax.ShapeDtypeStruct((8, rank), f32)]
        scratch += [
            pltpu.VMEM((2, tall, columns), f32),
            pltpu.VMEM((rows, rank), bf16),
            pltpu.VMEM((rows, rank), f32),
            pltpu.VMEM((col_size, 8, rank), f32),
            pltpu.SemaphoreType.DMA((2,)),
            pltpu.SemaphoreType.DMA((col_size - 1,)),
            pltpu.SemaphoreType.DMA((col_size - 1,)),
        ]
    return pl.pallas_call(
        functools.partial(project_kernel, col_size, step),
        out_shape=out_shape,
        in_specs=[hbm] * 3 + ([hbm, vmem] if step else []),
        out_specs=[vmem, hbm, vmem] if step else [vmem],
        scratch_shapes=scratch
        + [
            pltpu.VMEM(right.shape, f32),
            pltpu.SemaphoreType.DMA((2 + step, 2)),
            pltpu.SemaphoreType.DMA((bits + 1, blocks)),
            pltpu.SemaphoreType.DMA((bits + 1, blocks)),
            pltpu.SemaphoreType.DMA((1 + step,)),
        ],
        compiler_params=pltpu.CompilerParams(
            collective_id=collective_id, has_side_effects=True, vmem_limit_bytes=62 * 2**20
        ),
        cost_estimate=pl.CostEstimate(
            flops=8 * rows * columns * rank, bytes_accessed=10 * rows * columns, transcendentals=0
        ),
    )(*operands)


def finish_kernel(gain, buffer, ortho, raw, scale, left, right, before, change, state, lefts, highs, news, olds):
    c = pl.program_id(1)
    pieces = raw.shape[0]

    @pl.when((pl.program_id(0) == 0) & (c == 0))
    def _():
        lefts[0, 0], lefts[0, 1] = split(left[...] * (before[0:1, :] * gain))
        lefts[1, 0], lefts[1, 1] = split(ortho[...] * (scale[0:1, :] * gain))
        highs[...] = ortho[...].astype(jnp.bfloat16)

    @pl.when(pl.program_id(0) == 0)
    def _():
        for k in range(pieces):
            news[c * pieces + k, 0], news[c * pieces + k, 1] = split(raw[k])
            olds[c * pieces + k, 0], olds[c * pieces + k, 1] = split(right[k])

    dims = ((1,), (0,))
    tall = buffer.shape[0]
    here = pl.ds(pl.multiple_of(pl.program_id(0) * tall, tall), tall)
    for k in range(pieces):
        at = slice(k * WIDTH, (k + 1) * WIDTH)
        r_high, r_low = news[c * pieces + k, 0], news[c * pieces + k, 1]
        p_high, p_low = olds[c * pieces + k, 0], olds[c * pieces + k, 1]
        state[:, at] = buffer[:, at] - (1.0 - keep_rate) * matmul(highs[here, :], r_high, dims, None)
        total = matmul(lefts[0, 0, here, :], p_high, dims, None)
        total = total + matmul(lefts[0, 1, here, :], p_high, dims, None)
        total = total + matmul(lefts[0, 0, here, :], p_low, dims, None)
        total = total + matmul(lefts[1, 0, here, :], r_high, dims, None)
        total = total + matmul(lefts[1, 1, here, :], r_high, dims, None)
        total = total + matmul(lefts[1, 0, here, :], r_low, dims, None)
        change[:, at] = total.astype(jnp.bfloat16)


TILE_ROWS = 1024
TILE_PIECES = 2


def finish(gain, buffer, ortho, raw, scale, left, right, before):
    rows, columns = buffer.shape
    rank = ortho.shape[1]
    bf16 = jnp.bfloat16
    tall, pieces = min(TILE_ROWS, rows), min(TILE_PIECES, columns // WIDTH)
    tile = pl.BlockSpec((tall, pieces * WIDTH), lambda r, c: (r, c))
    last = columns // WIDTH // pieces - 1
    chunk = pl.BlockSpec((pieces, rank, WIDTH), lambda r, c: (jnp.where(r == 0, c, last), 0, 0))
    whole = pl.BlockSpec((rows, rank), lambda r, c: (0, 0))
    row = pl.BlockSpec((8, rank), lambda r, c: (0, 0))
    return pl.pallas_call(
        functools.partial(finish_kernel, gain),
        grid=(rows // tall, columns // WIDTH // pieces),
        out_shape=[
            jax.ShapeDtypeStruct((rows, columns), bf16),
            jax.ShapeDtypeStruct((rows, columns), jnp.float32),
        ],
        in_specs=[tile, whole, chunk, row, whole, chunk, row],
        out_specs=[tile, tile],
        scratch_shapes=[
            pltpu.VMEM((2, 2, rows, rank), bf16),
            pltpu.VMEM((rows, rank), bf16),
            pltpu.VMEM((columns // WIDTH, 2, rank, WIDTH), bf16),
            pltpu.VMEM((columns // WIDTH, 2, rank, WIDTH), bf16),
        ],
        compiler_params=pltpu.CompilerParams(vmem_limit_bytes=62 * 2**20),
        cost_estimate=pl.CostEstimate(
            flops=14 * rows * columns * rank, bytes_accessed=10 * rows * columns, transcendentals=0
        ),
    )(buffer, ortho, raw, scale, left, right, before)


def shards(row_size, col_size, momentum, grads, basis):
    rank = basis.shape[1]
    gain = (momentum.shape[0] * row_size * momentum.shape[1] * col_size / rank) ** 0.5
    (projected,) = project(momentum, grads, 0, basis, None, None, col_size, 0)
    left, right, norms = row_reduce(momentum, grads, 0, projected, row_size, col_size, 1)
    projected, buffer, before = project(momentum, grads, 1, right, left, norms, col_size, 2)
    ortho, raw, scale = row_reduce(buffer, None, None, projected, row_size, col_size, 3)
    return tuple(finish(gain, buffer, ortho, raw, scale, left, right, before))


def solution(mesh):
    return jax.shard_map(
        functools.partial(shards, mesh.shape["row"], mesh.shape["col"]),
        mesh=mesh,
        in_specs=(P("row", "col"), P(None, "row", "col"), P("col", None)),
        out_specs=(P("row", "col"), P("row", "col")),
        check_vma=False,
    )
```

```python
import functools

import jax
import jax.numpy as jnp
from jax import lax
from jax.experimental import pallas as pl
from jax.experimental.pallas import tpu as pltpu
from jax.sharding import PartitionSpec as P

keep_rate = 0.95
norm_eps = 1e-06
HIGH = lax.Precision.HIGH
HIGHEST = lax.Precision.HIGHEST
MESH = pl.DeviceIdType.MESH
LANES = 128
STRIDE = 2
SLOTS = 3
WIDTH = 256
LAG = 3
SHARE = 40
EXTRA = 1


def matmul(a, b, dims, precision):
    return lax.dot_general(a, b, (dims, ((), ())), precision=precision, preferred_element_type=jnp.float32)


def split(x):
    high = x.astype(jnp.bfloat16)
    return high, (x - high.astype(jnp.float32)).astype(jnp.bfloat16)


KINDS = 12


def shares(rank):
    size = rank * SHARE // 256 // 8 * 8
    return size, (rank - 4 * size) // 2


def inverse_norms(slots, cols):
    whole = slots[0]
    for d in range(1, cols):
        whole = whole + slots[d]
    return lax.rsqrt(whole + norm_eps)


def row_kernel(rows, cols, step, *refs):
    state, refs = refs[0], refs[1:]
    if step is not None:
        grads, refs = refs[0], refs[1:]
    projected, ortho, raw, scale, refs = *refs[:4], refs[4:]
    fin, work, upward, pair, turned, factor, panel, squares, slots, states, refs = *refs[:10], refs[10:]
    if step is not None:
        slopes, refs = refs[0], refs[1:]
    ortho_here, raw_here, load_sem, send_sem, recv_sem, norm_send, norm_recv, out_sem = refs
    line = rows // 2
    rank = factor.shape[0]
    first = rank // WIDTH
    chunks = fin.shape[0]
    size, wide = shares(rank)
    me = lax.axis_index("row")
    y = lax.rem(me, 2)
    z = me // 2
    partner = me + 1 - 2 * y
    mine = pl.multiple_of(2 * size * y, 8)
    yours = pl.multiple_of(2 * size * (1 - y), 8)
    away = (z, line - 1 - z)
    nearer = (me - 2, me + 2)
    farther = (me + 2, me - 2)
    one = tuple(pl.multiple_of(mine + size * p, 8) for p in range(2))
    two = tuple(4 * size + wide * p for p in range(2))

    def load(j, slot):
        columns = pl.ds(pl.multiple_of(j * WIDTH, WIDTH), WIDTH)
        copies = [pltpu.make_async_copy(state.at[:, columns], states.at[slot], load_sem.at[0, slot])]
        if step is not None:
            copies.append(pltpu.make_async_copy(grads.at[step, :, columns], slopes.at[slot], load_sem.at[1, slot]))
        return copies

    barrier = pltpu.get_barrier_semaphore()
    pl.semaphore_signal(barrier, inc=1, device_id={"row": partner}, device_id_type=MESH)
    for p in range(2):
        @pl.when(away[p] > 0)
        def _():
            pl.semaphore_signal(barrier, inc=1, device_id={"row": nearer[p]}, device_id_type=MESH)

    mine_col = lax.axis_index("col")
    others = [lax.rem(mine_col + d, cols) for d in range(1, cols)] if step is None else []
    for other in others:
        pl.semaphore_signal(barrier, inc=1, device_id={"col": other}, device_id_type=MESH)
    for j in range(SLOTS - 1):
        for copy in load(j, j):
            copy.start()

    def send(kind, c, source, start, target, at, count, device):
        return pltpu.make_async_remote_copy(
            src_ref=source.at[c, pl.ds(start, count)],
            dst_ref=target.at[c, pl.ds(at, count)],
            send_sem=send_sem.at[kind, c],
            recv_sem=recv_sem.at[kind, c],
            device_id={"row": device},
            device_id_type=MESH,
        )

    copies = {0: lambda c: send(0, c, work, yours, pair, 0, 2 * size, partner)}
    for p in range(2):
        n, f, o, t = nearer[p], farther[p], one[p], two[p]
        up = upward.at[p]
        copies[1 + p] = functools.partial(send, 1 + p, source=work, start=o, target=up, at=0, count=size, device=n)
        copies[3 + p] = functools.partial(
            send, 3 + p, source=work, start=t, target=up, at=size, count=wide, device=n
        )
        copies[6 + p] = functools.partial(send, 6 + p, source=fin, start=o, target=fin, at=o, count=size, device=f)
        copies[8 + p] = functools.partial(send, 8 + p, source=fin, start=t, target=fin, at=t, count=wide, device=f)
        copies[10 + p] = functools.partial(
            send, 10 + p, source=fin, start=o, target=fin, at=o, count=size, device=partner
        )
    cross = [
        functools.partial(
            send, 5, source=work, start=two[p], target=pair, at=2 * size, count=wide, device=partner
        )
        for p in range(2)
    ]

    def add(target, c, start, source, at, count):
        target[c, pl.ds(start, count), :] = work[c, pl.ds(start, count), :] + source[c, pl.ds(at, count), :]

    transposed = projected[...].T
    high, low = split(transposed)
    turned[0] = high
    turned[1] = low
    gram = matmul(transposed, transposed, ((1,), (1,)), HIGHEST)
    for k in range(first):
        work[k] = gram[:, k * WIDTH : (k + 1) * WIDTH]

    pl.semaphore_wait(barrier, jnp.where((z == 0) | (z == line - 1), 2, 3) + len(others))

    turn = line * STRIDE
    delay = max(turn, chunks + 1 - 2 * STRIDE + EXTRA) - turn
    last = 2 * turn + delay

    block = 32
    per = 16
    pieces = rank // per
    begin = 2 * turn + first

    def eliminate(t):
        k0 = (t * per // block) * block
        part = t % (block // per)
        tile = (k0 // LANES) * LANES
        shift = k0 % LANES
        r = lax.broadcasted_iota(jnp.int32, (block, LANES), 0)
        l = lax.broadcasted_iota(jnp.int32, (block, LANES), 1)
        if part == 0:
            d = factor[k0 : k0 + block, tile : tile + LANES]
            if shift:
                d = pltpu.roll(d, LANES - shift, 1)
            aug = jnp.where(l < block, d, jnp.where(l - block == r, 1.0, 0.0))
        else:
            aug = panel[...]
        for j in range(part * per, (part + 1) * per):
            column = jnp.broadcast_to(aug[:, j : j + 1], (block, LANES))
            pivot = column[j : j + 1, :]
            ratio = jnp.where(r > j, column * (1.0 / pivot), 0.0)
            aug = aug - ratio * aug[j : j + 1, :]
        if part < block // per - 1:
            panel[...] = aug
            return
        diagonal = jnp.sum(jnp.where(l == r, aug, 0.0), axis=1, keepdims=True)
        t_inv = (aug * lax.rsqrt(diagonal))[:, block : 2 * block]
        rw = lax.broadcasted_iota(jnp.int32, (block, rank), 0)
        lw = lax.broadcasted_iota(jnp.int32, (block, rank), 1)
        inside = (lw >= k0) & (lw < k0 + block)
        own = jnp.where(inside, jnp.where(lw - k0 == rw, 1.0, 0.0), factor[k0 : k0 + block, :])
        done = matmul(t_inv, own, ((1,), (0,)), HIGHEST)
        factor[k0 : k0 + block, :] = done
        rest = rank - k0 - block
        if rest:
            below = factor[k0 + block :, :]
            left_part = matmul(below[:, k0 : k0 + block], t_inv, ((1,), (1,)), HIGHEST)
            lb = lax.broadcasted_iota(jnp.int32, (rest, rank), 1)
            kept = jnp.where((lb >= k0) & (lb < k0 + block), 0.0, below)
            factor[k0 + block :, :] = kept - matmul(left_part, done, ((1,), (0,)), HIGHEST)

    def finish():
        r = lax.broadcasted_iota(jnp.int32, (rank, rank), 0)
        l = lax.broadcasted_iota(jnp.int32, (rank, rank), 1)
        inverse = jnp.where(l <= r, factor[...], 0.0)
        high, low = split(inverse)
        turned[0, :, :rank] = high
        turned[1, :, :rank] = low
        ortho_here[...] = matmul(projected[...], inverse, ((1,), (1,)), HIGHEST)
        pltpu.make_async_copy(ortho_here, ortho, out_sem.at[chunks - first]).start()
        squares[...] = jnp.zeros_like(squares)

    def expand(c):
        t_high, t_low = split(fin[c])
        i_high, i_low = turned[0, :, :rank], turned[1, :, :rank]
        dims = ((1,), (0,))
        value = matmul(i_high, t_high, dims, None) + matmul(i_high, t_low, dims, None) + matmul(i_low, t_high, dims, None)
        raw_here[c - first] = value
        pltpu.make_async_copy(raw_here.at[c - first], raw.at[c - first], out_sem.at[c - first]).start()
        square = value * value
        squares[...] += sum(square[:, k : k + LANES] for k in range(0, WIDTH, LANES))

    total = chunks + last
    ready = max(begin + pieces, chunks)

    def reached(i):
        count = jnp.minimum(jnp.minimum(first + 3 * (i - ready + 1), i - (last - 1) + 1), chunks)
        return jnp.maximum(count, first)

    @pl.loop(0, total)
    def _(i):
        @pl.when(i < chunks)
        def _():
            c = i

            @pl.when(c >= first)
            def _():
                j = c - first
                slot = lax.rem(j, SLOTS)
                ahead = j + SLOTS - 1

                @pl.when(ahead < chunks - first)
                def _():
                    for copy in load(ahead, lax.rem(ahead, SLOTS)):
                        copy.start()

                for copy in load(j, slot):
                    copy.wait()
                buffer = states[slot]
                if step is not None:
                    buffer = buffer + slopes[slot].astype(jnp.float32)
                b_high, b_low = split(buffer)
                dims = ((1,), (0,))
                work[c] = (
                    matmul(turned[0], b_high, dims, None)
                    + matmul(turned[0], b_low, dims, None)
                    + matmul(turned[1], b_high, dims, None)
                )

            copies[0](c).start()

        def stage(offset, action, when=True, low=0, high=chunks):
            c = i - offset

            @pl.when((c >= low) & (c < high) & when)
            def _():
                action(c)

        def paired(c):
            copies[0](c).wait_recv()
            add(work, c, mine, pair, 0, 2 * size)

        def rise_one(c, p):
            @pl.when(away[p] < line - 1)
            def _():
                copies[1 + p](c).wait_recv()

                @pl.when(away[p] > 0)
                def _():
                    add(work, c, one[p], upward.at[p], 0, size)

                @pl.when(away[p] == 0)
                def _():
                    add(fin, c, one[p], upward.at[p], 0, size)

            @pl.when(away[p] > 0)
            def _():
                copies[1 + p](c).start()

        def rise_two(c, p):
            @pl.when(away[p] < line - 1)
            def _():
                copies[3 + p](c).wait_recv()
                add(work, c, two[p], upward.at[p], size, wide)

            @pl.when(away[p] > 0)
            def _():
                copies[3 + p](c).start()

        def exchange(c, p):
            cross[p](c).start()

        def crossed(c, p):
            cross[p](c).wait_recv()
            add(fin, c, two[p], pair, 2 * size, wide)

        def fall(c, p):
            @pl.when(away[p] > 0)
            def _():
                copies[6 + p](c).wait_recv()

            @pl.when(away[p] < line - 1)
            def _():
                copies[6 + p](c).start()

            copies[10 + p](c).start()

            @pl.when(away[p] > 0)
            def _():
                copies[8 + p](c).wait_recv()

            @pl.when(away[p] < line - 1)
            def _():
                copies[8 + p](c).start()

        def gathered(c):
            copies[10](c).wait_recv()
            copies[11](c).wait_recv()

        stage(STRIDE, paired)
        for p in range(2):
            height = (line - 1 - away[p]) * STRIDE
            stage(height, functools.partial(rise_two, p=p))
            stage(STRIDE + height, functools.partial(rise_one, p=p))
        for low, high, later in ((0, first, 0), (first, chunks, delay)):
            for p in range(2):
                at = turn - STRIDE + later // 2
                stage(at, functools.partial(exchange, p=p), away[p] == 0, low, high)
                stage(at + STRIDE, functools.partial(crossed, p=p), away[p] == 0, low, high)
                stage(turn + later + away[p] * STRIDE, functools.partial(fall, p=p), True, low, high)
            stage(2 * turn + later - 1, gathered, True, low, high)

        for t in range(pieces):
            @pl.when(i == begin + t)
            def _():
                if t == 0:
                    gram = jnp.concatenate([fin[k] for k in range(first)], axis=1)
                    factor[...] = 0.5 * (gram + gram.T)
                eliminate(t)

        if ready < total:
            @pl.when(i == ready)
            def _():
                finish()

            @pl.when(i >= ready)
            def _():
                @pl.loop(reached(i - 1), reached(i))
                def _(c):
                    expand(c)

    for t in range(pieces):
        if total <= begin + t:
            if t == 0:
                gram = jnp.concatenate([fin[k] for k in range(first)], axis=1)
                factor[...] = 0.5 * (gram + gram.T)
            eliminate(t)
    if total <= ready:
        finish()

    done = min(max(first + 3 * (total - ready), first), chunks) if ready < total else first

    @pl.loop(done, chunks)
    def _(c):
        expand(c)

    own = matmul(jnp.ones((8, LANES), jnp.float32), squares[...], ((1,), (1,)), HIGHEST)
    if step is None:
        slots[mine_col] = own
    else:
        scale[...] = own
    norms = [
        pltpu.make_async_remote_copy(
            src_ref=slots.at[mine_col],
            dst_ref=slots.at[mine_col],
            send_sem=norm_send.at[d],
            recv_sem=norm_recv.at[d],
            device_id={"col": other},
            device_id_type=MESH,
        )
        for d, other in enumerate(others)
    ]
    for copy in norms:
        copy.start()

    @pl.loop(0, chunks)
    def _(c):
        for kind in (0, 10, 11):
            copies[kind](c).wait_send()
        for p in range(2):
            @pl.when(away[p] > 0)
            def _():
                copies[1 + p](c).wait_send()
                copies[3 + p](c).wait_send()

            @pl.when(away[p] == 0)
            def _():
                cross[p](c).wait_send()

            @pl.when(away[p] < line - 1)
            def _():
                copies[6 + p](c).wait_send()
                copies[8 + p](c).wait_send()

    pltpu.make_async_copy(ortho_here, ortho, out_sem.at[chunks - first]).wait()

    @pl.loop(0, chunks - first)
    def _(c):
        pltpu.make_async_copy(raw_here.at[c], raw.at[c], out_sem.at[c]).wait()

    if step is None:
        for copy in norms:
            copy.wait()
        scale[...] = inverse_norms(slots, cols)


def row_reduce(state, grads, step, projected, row_size, col_size, collective_id):
    rows, columns = state.shape
    rank = projected.shape[1]
    chunks = (columns + rank) // WIDTH
    vmem = pl.BlockSpec(memory_space=pltpu.VMEM)
    hbm = pl.BlockSpec(memory_space=pltpu.HBM)
    size, wide = shares(rank)
    f32 = jnp.float32
    operands = (state, projected) if step is None else (state, grads, projected)
    return pl.pallas_call(
        functools.partial(row_kernel, row_size, col_size, step),
        out_shape=[
            jax.ShapeDtypeStruct((rows, rank), f32),
            jax.ShapeDtypeStruct((columns // WIDTH, rank, WIDTH), f32),
            jax.ShapeDtypeStruct((8, rank), f32),
        ],
        in_specs=[hbm] * (len(operands) - 1) + [vmem],
        out_specs=[hbm, hbm, vmem],
        scratch_shapes=[
            pltpu.VMEM((chunks, rank, WIDTH), f32),
            pltpu.VMEM((chunks, rank, WIDTH), f32),
            pltpu.VMEM((2, chunks, size + wide, WIDTH), f32),
            pltpu.VMEM((chunks, 2 * size + wide, WIDTH), f32),
            pltpu.VMEM((2, rank, rows), jnp.bfloat16),
            pltpu.VMEM((rank, rank), f32),
            pltpu.VMEM((32, LANES), f32),
            pltpu.VMEM((rank, LANES), f32),
            pltpu.VMEM((col_size, 8, rank), f32),
            pltpu.VMEM((SLOTS, rows, WIDTH), f32),
        ]
        + ([] if step is None else [pltpu.VMEM((SLOTS, rows, WIDTH), jnp.bfloat16)])
        + [
            pltpu.VMEM((rows, rank), f32),
            pltpu.VMEM((columns // WIDTH, rank, WIDTH), f32),
            pltpu.SemaphoreType.DMA((2, SLOTS)),
            pltpu.SemaphoreType.DMA((KINDS, chunks)),
            pltpu.SemaphoreType.DMA((KINDS, chunks)),
            pltpu.SemaphoreType.DMA((col_size - 1,)),
            pltpu.SemaphoreType.DMA((col_size - 1,)),
            pltpu.SemaphoreType.DMA((columns // WIDTH + 1,)),
        ],
        compiler_params=pltpu.CompilerParams(
            collective_id=collective_id, has_side_effects=True, vmem_limit_bytes=62 * 2**20
        ),
        cost_estimate=pl.CostEstimate(
            flops=6 * rows * columns * rank, bytes_accessed=6 * rows * columns, transcendentals=0
        ),
    )(*operands)


def project_kernel(cols, step, *refs):
    state, grads, right, refs = *refs[:3], refs[3:]
    if step:
        ortho, norms, refs = *refs[:2], refs[2:]
    projected, refs = refs[0], refs[1:]
    if step:
        buffer, scale, refs = *refs[:2], refs[2:]
    states, slopes, high, low, part, pair, sums, recvs, refs = *refs[:8], refs[8:]
    if step:
        buffers, left, ortho_here, slots, store_sem, norm_send, norm_recv, refs = *refs[:7], refs[7:]
    right_here, load_sem, send_sem, recv_sem, right_sem = refs
    tall = states.shape[1]
    rows, rank = projected.shape
    columns = state.shape[1]
    blocks = rows // tall
    half = tall // 2
    bits = cols.bit_length() - 1
    me = lax.axis_index("col")
    partners = [me + (1 - 2 * lax.rem(me // (1 << b), 2)) * (1 << b) for b in range(bits)]
    mine = pl.multiple_of(half * lax.rem(me, 2), 8)
    yours = pl.multiple_of(half * (1 - lax.rem(me, 2)), 8)

    def load(r):
        where = pl.ds(r * tall, tall)
        slot = r % 2
        copies = [pltpu.make_async_copy(state.at[where], states.at[slot], load_sem.at[0, slot])]
        for g in range(step + 1):
            copies.append(
                pltpu.make_async_copy(grads.at[g, where], slopes.at[slot, g], load_sem.at[1 + g, slot])
            )
        return copies

    fetch = [pltpu.make_async_copy(right, right_here, right_sem.at[0])]
    if step:
        fetch.append(pltpu.make_async_copy(ortho, ortho_here, right_sem.at[1]))
    for copy in fetch + load(0) + (load(1) if blocks > 1 else []):
        copy.start()

    barrier = pltpu.get_barrier_semaphore()
    others = [lax.rem(me + d, cols) for d in range(1, cols)] if step else []
    for other in others if step else partners:
        pl.semaphore_signal(barrier, inc=1, device_id={"col": other}, device_id_type=MESH)

    for copy in fetch:
        copy.wait()
    if step:
        for c in range(columns // WIDTH):
            at = slice(c * WIDTH, (c + 1) * WIDTH)
            high[:, at], low[:, at] = split(right_here[c])
        left[...] = ortho_here[...].astype(jnp.bfloat16)
    else:
        high[...], low[...] = split(right_here[...])

    pl.semaphore_wait(barrier, len(others) if step else bits)
    exchange = [
        pltpu.make_async_remote_copy(
            src_ref=norms,
            dst_ref=slots.at[me],
            send_sem=norm_send.at[d],
            recv_sem=norm_recv.at[d],
            device_id={"col": other},
            device_id_type=MESH,
        )
        for d, other in enumerate(others)
    ]
    for copy in exchange:
        copy.start()
    if step:
        slots[me] = norms[...]

    def remote(kind, r, source, target, partner):
        return pltpu.make_async_remote_copy(
            src_ref=source,
            dst_ref=target,
            send_sem=send_sem.at[kind, r],
            recv_sem=recv_sem.at[kind, r],
            device_id={"col": partner},
            device_id_type=MESH,
        )

    def swap(r):
        return remote(0, r, part.at[r, pl.ds(yours, half)], pair.at[r], partners[0])

    def cross(b, r):
        return remote(b, r, sums.at[b - 1, r], recvs.at[b - 1, r], partners[b])

    def whole(r):
        return projected.at[pl.ds(pl.multiple_of(r * tall + mine, 8), half)]

    def gather(r):
        return remote(bits, r, whole(r), whole(r), partners[0])

    def arrive(k, r):
        if k == 1:
            swap(r).wait_recv()
            value = part[r, pl.ds(mine, half), :] + pair[r]
        else:
            cross(k - 1, r).wait_recv()
            value = sums[k - 2, r] + recvs[k - 2, r]
        if k < bits:
            sums[k - 1, r] = value
            cross(k, r).start()
        else:
            if step:
                value = value * scale[0:1, :]
            whole(r)[...] = value
            gather(r).start()

    deep = min(columns, 2048)
    due = {1 + LAG * (k - 1): k for k in range(1, bits + 1)}
    for t in range(blocks + max(due)):
        if t < blocks:
            slot = t % 2
            if 1 <= t < blocks - 1:
                for copy in load(t + 1):
                    copy.start()
            for copy in load(t):
                copy.wait()
            if step and t >= 2:
                store(t - 2).wait()
            part[t] = jnp.zeros(part.shape[1:], jnp.float32)

            @pl.loop(0, columns // deep)
            def _(k):
                at = pl.ds(pl.multiple_of(k * deep, deep), deep)
                value = states[slot, :, at] + slopes[slot, 0, :, at].astype(jnp.float32)
                if step:
                    update = matmul(left[t * tall : (t + 1) * tall, :], high[:, at], ((1,), (0,)), None)
                    value = value - (1.0 - keep_rate) * update
                    value = value + slopes[slot, 1, :, at].astype(jnp.float32)
                    buffers[slot, :, at] = value
                    r_high, r_low, dims = high[:, at], low[:, at], ((1,), (1,))
                else:
                    r_high, r_low, dims = high[at, :], low[at, :], ((1,), (0,))
                v_high, v_low = split(value)
                part[t] += (
                    matmul(v_high, r_high, dims, None)
                    + matmul(v_low, r_high, dims, None)
                    + matmul(v_high, r_low, dims, None)
                )

            if step:
                def store(r):
                    return pltpu.make_async_copy(
                        buffers.at[r % 2], buffer.at[pl.ds(r * tall, tall)], store_sem.at[r % 2]
                    )

                store(t).start()
            swap(t).start()
            if step and t == 0:
                for copy in exchange:
                    copy.wait()
                scale[...] = inverse_norms(slots, cols)
        for r in range(blocks):
            if t - r in due:
                arrive(due[t - r], r)

    for r in range(blocks):
        swap(r).wait_send()
        gather(r).wait()
        for b in range(1, bits):
            cross(b, r).wait_send()
        if step and r >= blocks - 2:
            store(r).wait()


def project(state, grads, step, right, ortho, norms, col_size, collective_id):
    rows, columns = state.shape
    rank = right.shape[1]
    tall = min(256 if step else 128, rows)
    blocks = rows // tall
    bits = col_size.bit_length() - 1
    vmem = pl.BlockSpec(memory_space=pltpu.VMEM)
    hbm = pl.BlockSpec(memory_space=pltpu.HBM)
    f32, bf16 = jnp.float32, jnp.bfloat16
    operands = (state, grads, right) + ((ortho, norms) if step else ())
    shape = (rank, columns) if step else (columns, rank)
    out_shape = [jax.ShapeDtypeStruct((rows, rank), f32)]
    scratch = [
        pltpu.VMEM((2, tall, columns), f32),
        pltpu.VMEM((2, step + 1, tall, columns), bf16),
        pltpu.VMEM(shape, bf16),
        pltpu.VMEM(shape, bf16),
        pltpu.VMEM((blocks, tall, rank), f32),
        pltpu.VMEM((blocks, tall // 2, rank), f32),
        pltpu.VMEM((bits - 1, blocks, tall // 2, rank), f32),
        pltpu.VMEM((bits - 1, blocks, tall // 2, rank), f32),
    ]
    if step:
        out_shape += [jax.ShapeDtypeStruct((rows, columns), f32), jax.ShapeDtypeStruct((8, rank), f32)]
        scratch += [
            pltpu.VMEM((2, tall, columns), f32),
            pltpu.VMEM((rows, rank), bf16),
            pltpu.VMEM((rows, rank), f32),
            pltpu.VMEM((col_size, 8, rank), f32),
            pltpu.SemaphoreType.DMA((2,)),
            pltpu.SemaphoreType.DMA((col_size - 1,)),
            pltpu.SemaphoreType.DMA((col_size - 1,)),
        ]
    return pl.pallas_call(
        functools.partial(project_kernel, col_size, step),
        out_shape=out_shape,
        in_specs=[hbm] * 3 + ([hbm, vmem] if step else []),
        out_specs=[vmem, hbm, vmem] if step else [vmem],
        scratch_shapes=scratch
        + [
            pltpu.VMEM(right.shape, f32),
            pltpu.SemaphoreType.DMA((2 + step, 2)),
            pltpu.SemaphoreType.DMA((bits + 1, blocks)),
            pltpu.SemaphoreType.DMA((bits + 1, blocks)),
            pltpu.SemaphoreType.DMA((1 + step,)),
        ],
        compiler_params=pltpu.CompilerParams(
            collective_id=collective_id, has_side_effects=True, vmem_limit_bytes=62 * 2**20
        ),
        cost_estimate=pl.CostEstimate(
            flops=8 * rows * columns * rank, bytes_accessed=10 * rows * columns, transcendentals=0
        ),
    )(*operands)


def finish_kernel(gain, buffer, ortho, raw, scale, left, right, before, change, state, lefts, highs, news, olds):
    c = pl.program_id(1)
    pieces = raw.shape[0]

    @pl.when((pl.program_id(0) == 0) & (c == 0))
    def _():
        lefts[0, 0], lefts[0, 1] = split(left[...] * (before[0:1, :] * gain))
        lefts[1, 0], lefts[1, 1] = split(ortho[...] * (scale[0:1, :] * gain))
        highs[...] = ortho[...].astype(jnp.bfloat16)

    @pl.when(pl.program_id(0) == 0)
    def _():
        for k in range(pieces):
            news[c * pieces + k, 0], news[c * pieces + k, 1] = split(raw[k])
            olds[c * pieces + k, 0], olds[c * pieces + k, 1] = split(right[k])

    dims = ((1,), (0,))
    tall = buffer.shape[0]
    here = pl.ds(pl.multiple_of(pl.program_id(0) * tall, tall), tall)
    for k in range(pieces):
        at = slice(k * WIDTH, (k + 1) * WIDTH)
        r_high, r_low = news[c * pieces + k, 0], news[c * pieces + k, 1]
        p_high, p_low = olds[c * pieces + k, 0], olds[c * pieces + k, 1]
        state[:, at] = buffer[:, at] - (1.0 - keep_rate) * matmul(highs[here, :], r_high, dims, None)
        total = matmul(lefts[0, 0, here, :], p_high, dims, None)
        total = total + matmul(lefts[0, 1, here, :], p_high, dims, None)
        total = total + matmul(lefts[0, 0, here, :], p_low, dims, None)
        total = total + matmul(lefts[1, 0, here, :], r_high, dims, None)
        total = total + matmul(lefts[1, 1, here, :], r_high, dims, None)
        total = total + matmul(lefts[1, 0, here, :], r_low, dims, None)
        change[:, at] = total.astype(jnp.bfloat16)


TILE_ROWS = 1024
TILE_PIECES = 2


def finish(gain, buffer, ortho, raw, scale, left, right, before):
    rows, columns = buffer.shape
    rank = ortho.shape[1]
    bf16 = jnp.bfloat16
    tall, pieces = min(TILE_ROWS, rows), min(TILE_PIECES, columns // WIDTH)
    tile = pl.BlockSpec((tall, pieces * WIDTH), lambda r, c: (r, c))
    last = columns // WIDTH // pieces - 1
    chunk = pl.BlockSpec((pieces, rank, WIDTH), lambda r, c: (jnp.where(r == 0, c, last), 0, 0))
    whole = pl.BlockSpec((rows, rank), lambda r, c: (0, 0))
    row = pl.BlockSpec((8, rank), lambda r, c: (0, 0))
    return pl.pallas_call(
        functools.partial(finish_kernel, gain),
        grid=(rows // tall, columns // WIDTH // pieces),
        out_shape=[
            jax.ShapeDtypeStruct((rows, columns), bf16),
            jax.ShapeDtypeStruct((rows, columns), jnp.float32),
        ],
        in_specs=[tile, whole, chunk, row, whole, chunk, row],
        out_specs=[tile, tile],
        scratch_shapes=[
            pltpu.VMEM((2, 2, rows, rank), bf16),
            pltpu.VMEM((rows, rank), bf16),
            pltpu.VMEM((columns // WIDTH, 2, rank, WIDTH), bf16),
            pltpu.VMEM((columns // WIDTH, 2, rank, WIDTH), bf16),
        ],
        compiler_params=pltpu.CompilerParams(vmem_limit_bytes=62 * 2**20),
        cost_estimate=pl.CostEstimate(
            flops=14 * rows * columns * rank, bytes_accessed=10 * rows * columns, transcendentals=0
        ),
    )(buffer, ortho, raw, scale, left, right, before)


def shards(row_size, col_size, momentum, grads, basis):
    rank = basis.shape[1]
    gain = (momentum.shape[0] * row_size * momentum.shape[1] * col_size / rank) ** 0.5
    (projected,) = project(momentum, grads, 0, basis, None, None, col_size, 0)
    left, right, norms = row_reduce(momentum, grads, 0, projected, row_size, col_size, 1)
    projected, buffer, before = project(momentum, grads, 1, right, left, norms, col_size, 2)
    ortho, raw, scale = row_reduce(buffer, None, None, projected, row_size, col_size, 3)
    return tuple(finish(gain, buffer, ortho, raw, scale, left, right, before))


def solution(mesh):
    return jax.shard_map(
        functools.partial(shards, mesh.shape["row"], mesh.shape["col"]),
        mesh=mesh,
        in_specs=(P("row", "col"), P(None, "row", "col"), P("col", None)),
        out_specs=(P("row", "col"), P("row", "col")),
        check_vma=False,
    )
```
